128 devices in a mesh: head: 8 (over z, core), query: 8 (over x, y_lo), ctx: 2 (over y_hi).
Axes of the slice: x: 4, y: 4 (y_hi: 2, y_lo: 2; y = y_hi * 2 + y_lo), z: 4, core: 2. Of those that a mesh axis runs over, the one named last changes fastest.
Arguments:
- queries: bfloat16 [1024, 128, 576], P('query', 'head'), may hold values from -3 to 3, as said below
- latent: bfloat16 [4096, 576], P(('head', 'query', 'ctx')), may hold values from -8 to 8
- out_grad: bfloat16 [1024, 128, 512], P('query', 'head'), may hold values from -6 to 6
- log_norms: float32 [1024, 128], P('query', 'head'), as said below
- row_dots: float32 [1024, 128], P('query', 'head'), may hold values from -48 to 48
Outputs:
- query_grad: float32 [1024, 128, 576], P(('query', 'ctx'), 'head')
- latent_grad: float32 [4096, 576], P(('head', 'query', 'ctx'))
The draws below stay inside these ranges and needn't reach their ends.
Inputs may be any that keep to these rules, and one draw needn't show every extreme that they name: queries and latent are of order one; latent rows may differ in scale. log_norms[i,h] is the log of the sum over all 4096 latent rows of exp(scores[i,h,j]), computed from the given queries and latent.
All inputs are finite; a program needn't handle non-finite values.
Results may differ from the reference program's by a relative error of at most 0.0029.
Values may be sent and summed in bfloat16 or wider, within the bound.
No kernel may reach another device: no remote copies, remote signals or barrier semaphores. Data moves between devices by JAX's collectives and lax.ppermute only.
A program may use at most 64 MiB of HBM per device.

```python
import math
import jax
import jax.numpy as jnp
from jax import lax

H = 128
DV = 512
DK = 576
Q = 1024
L = 4096


softmax_scale = 192.0 ** (-0.5) * (0.1 * math.log(40.0) + 1.0) ** 2


def shared_fields(key):
    query_key = jax.random.fold_in(key, 11)
    latent_key = jax.random.fold_in(key, 23)
    queries = jnp.clip(0.5 * jax.random.normal(query_key, (Q, H, DK), jnp.float32), -3.0, 3.0)
    latent = jnp.clip(jax.random.normal(latent_key, (L, DK), jnp.float32), -4.0, 4.0)
    return (queries.astype(jnp.bfloat16), latent.astype(jnp.bfloat16))


def draw_queries(key, part):
    return shared_fields(key)[0]


def draw_latent(key, part):
    return shared_fields(key)[1]


def draw_log_norms(key, part):
    queries, latent = shared_fields(key)
    flat_q = queries.reshape(Q * H, DK)
    row_block = min(4096, Q * H)

    def per_block(block_rows):
        scores = lax.dot_general(block_rows, latent, (((1,), (1,)), ((), ())), preferred_element_type=jnp.float32) * softmax_scale
        highest = jnp.max(scores, axis=1, keepdims=True)
        return (highest + jnp.log(jnp.sum(jnp.exp(scores - highest), axis=1, keepdims=True)))[:, 0]
    blocks_all = flat_q.reshape(Q * H // row_block, row_block, DK)
    return lax.map(per_block, blocks_all).reshape(Q, H).astype(jnp.float32)


def block_levels(rng, dims, split, low, largest):
    gain = 1.0
    for position, shards_of in split:
        heights = jax.random.uniform(jax.random.fold_in(jax.random.fold_in(rng, 6), position), (shards_of,), jnp.float32, low / len(split), largest / len(split))
        gain = gain * jnp.repeat(jnp.exp(heights), dims[position] // shards_of).reshape((-1,) + (1,) * (len(dims) - 1 - position))
    return gain


def gaussian(key, extent, width, bound, cuts=(), held_as=jnp.bfloat16):
    loudness = block_levels(key, extent, cuts, -0.22, 0.18) if cuts else 1.0
    array = jax.random.normal(key, extent, jnp.float32) * width * loudness
    return jnp.minimum(jnp.maximum(array, -bound), bound).astype(held_as)


def setup_inputs(seed: int = 0) -> dict:
    key_of = jax.random.split(jax.random.key(seed), 6)
    return {
        "queries": draw_queries(jax.random.fold_in(key_of[5], 71), 0),
        "latent": draw_latent(jax.random.fold_in(key_of[5], 71), 0),
        "out_grad": gaussian(key_of[2], (Q, H, DV), 1.0, 6.0, ((0, 8), (1, 8))),
        "log_norms": draw_log_norms(jax.random.fold_in(key_of[5], 71), 0),
        "row_dots": gaussian(key_of[4], (Q, H), 8.0, 48.0, ((0, 8), (1, 8)), jnp.float32),
    }


softmax_scale = 192.0 ** -0.5 * (0.1 * math.log(40.0) + 1.0) ** 2


def reference(queries, latent, out_grad, log_norms, row_dots):
    head_group = 8
    group_count = H // head_group
    value_latent = latent[:, :DV]

    def per_group(index):
        first = index * head_group
        group_q = lax.dynamic_slice_in_dim(queries, first, head_group, 1).reshape(Q * head_group, DK)
        group_dout = lax.dynamic_slice_in_dim(out_grad, first, head_group, 1).reshape(Q * head_group, DV)
        norms = lax.dynamic_slice_in_dim(log_norms, first, head_group, 1).reshape(Q * head_group)
        dots = lax.dynamic_slice_in_dim(row_dots, first, head_group, 1).reshape(Q * head_group)
        scores = lax.dot_general(group_q, latent, (((1,), (1,)), ((), ())), preferred_element_type=jnp.float32) * softmax_scale
        probs = jnp.exp(scores - norms[:, None])
        probs_low = probs.astype(jnp.bfloat16)
        dprobs = lax.dot_general(group_dout, value_latent, (((1,), (1,)), ((), ())), preferred_element_type=jnp.float32)
        dscores = (probs * (dprobs - dots[:, None])).astype(jnp.bfloat16)
        query_part = jnp.dot(dscores, latent, preferred_element_type=jnp.float32) * softmax_scale
        latent_key = lax.dot_general(dscores, group_q, (((0,), (0,)), ((), ())), preferred_element_type=jnp.float32) * softmax_scale
        latent_value = lax.dot_general(probs_low, group_dout, (((0,), (0,)), ((), ())), preferred_element_type=jnp.float32)
        latent_part = latent_key + jnp.pad(latent_value, ((0, 0), (0, DK - DV)))
        return query_part.reshape(Q, head_group, DK), latent_part

    query_parts, latent_parts = lax.map(per_group, jnp.arange(group_count, dtype=jnp.int32))
    query_grad = jnp.transpose(query_parts, (1, 0, 2, 3)).reshape(Q, H, DK)
    latent_grad = jnp.sum(latent_parts, axis=0)
    return query_grad, latent_grad
```

```python
import functools
import math

import jax
import jax.numpy as jnp
from jax import lax
from jax.experimental import pallas as pl
from jax.experimental.pallas import tpu as pltpu
from jax.sharding import Mesh, PartitionSpec as P

softmax_scale = 192.0 ** (-0.5) * (0.1 * math.log(40.0) + 1.0) ** 2
log2_e = math.log2(math.e)

FINE_AXES = ("z", "core", "x", "y_lo", "y_hi")
CHIP_AXES = ("z", "x", "y_lo", "y_hi")
CHUNKS = (16, 16)
TILE = 256

NT = (((1,), (1,)), ((), ()))
NN = (((1,), (0,)), ((), ()))
TN = (((0,), (0,)), ((), ()))


def f32_dot(left, right, dims):
    return lax.dot_general(left, right, dims, preferred_element_type=jnp.float32)


def chunk_kernel(first, *refs):
    if first:
        k_ref, q_ref, do_ref, norm_ref, dot_ref, dkv_ref, dq_ref, key_acc, value_acc = refs
    else:
        k_ref, q_ref, do_ref, norm_ref, dot_ref, dq_in_ref, dkv_ref, dq_ref, key_acc, value_acc = refs
    step = pl.program_id(0)
    width = do_ref.shape[1]

    @pl.when(step == 0)
    def _():
        key_acc[...] = jnp.zeros_like(key_acc)
        value_acc[...] = jnp.zeros_like(value_acc)

    keys = k_ref[...]
    queries = q_ref[...]
    douts = do_ref[...]
    scores = f32_dot(keys, queries, NT)
    dprobs = f32_dot(keys[:, :width], douts, NT)
    probs = jnp.exp2(scores * (softmax_scale * log2_e) - norm_ref[...] * log2_e)
    dscores = (probs * (dprobs - dot_ref[...])).astype(jnp.bfloat16)
    query_part = f32_dot(dscores, keys, TN)
    dq_ref[...] = query_part if first else dq_in_ref[...] + query_part
    key_acc[...] += f32_dot(dscores, queries, NN)
    value_acc[...] += f32_dot(probs.astype(jnp.bfloat16), douts, NN)

    @pl.when(step == pl.num_programs(0) - 1)
    def _():
        dkv_ref[:, :width] = (key_acc[:, :width] * softmax_scale + value_acc[...]).astype(dkv_ref.dtype)
        dkv_ref[:, width:] = (key_acc[:, width:] * softmax_scale).astype(dkv_ref.dtype)


def chunk_grads(keys, queries, douts, norms, dots, dq):
    rows, key_width = keys.shape
    total, width = douts.shape
    first = dq is None
    whole = pl.BlockSpec((rows, key_width), lambda i: (0, 0))
    tile = lambda n: pl.BlockSpec((TILE, n), lambda i: (i, 0))
    row = pl.BlockSpec((1, TILE), lambda i: (0, i))
    in_specs = [whole, tile(key_width), tile(width), row, row]
    operands = [keys, queries, douts, norms, dots]
    if not first:
        in_specs.append(tile(key_width))
        operands.append(dq)
    flops = 2 * rows * total * (3 * key_width + 2 * width)
    moved = total * (key_width * 2 + width * 2 + key_width * (4 if first else 8)) + rows * key_width * 4
    return pl.pallas_call(
        functools.partial(chunk_kernel, first),
        grid=(total // TILE,),
        in_specs=in_specs,
        out_specs=[whole, tile(key_width)],
        out_shape=[
            jax.ShapeDtypeStruct((rows, key_width), jnp.bfloat16),
            jax.ShapeDtypeStruct((total, key_width), jnp.float32),
        ],
        scratch_shapes=[
            pltpu.VMEM((rows, key_width), jnp.float32),
            pltpu.VMEM((rows, width), jnp.float32),
        ],
        input_output_aliases={} if first else {5: 1},
        compiler_params=pltpu.CompilerParams(vmem_limit_bytes=48 << 20),
        cost_estimate=pl.CostEstimate(flops=flops, bytes_accessed=moved, transcendentals=rows * total),
        name="chunk_grads",
    )(*operands)


def on_device(queries, latent, out_grad, log_norms, row_dots):
    key_width = queries.shape[2]
    heads = queries.shape[1]
    chips = lax.axis_size(CHIP_AXES)
    half = queries.shape[0] // lax.axis_size("y_hi")

    def gather(start, rows):
        piece = lax.slice_in_dim(latent, start, start + rows, axis=0)
        spread = jnp.broadcast_to(piece[None], (chips, rows, key_width))
        got = lax.all_to_all(spread, CHIP_AXES, 0, 0, tiled=True)
        return got.reshape(chips * rows, key_width)

    starts = [sum(CHUNKS[:n]) for n in range(len(CHUNKS))]
    gathered = [gather(start, rows) for start, rows in zip(starts, CHUNKS)]

    def both(array):
        first = lax.axis_index("y_hi") * half
        mine = lax.dynamic_slice_in_dim(array, first, half, axis=0)
        theirs = lax.ppermute(mine, "core", [(0, 1), (1, 0)])
        return jnp.concatenate([mine.reshape((half * heads,) + mine.shape[2:]), theirs.reshape((half * heads,) + mine.shape[2:])])

    flat_q = both(queries)
    flat_dout = both(out_grad)
    stats = both(jnp.stack([log_norms, row_dots], axis=-1))
    norms = stats[:, 0][None]
    dots = stats[:, 1][None]

    dq = None
    latent_parts = []
    for rows, keys in zip(CHUNKS, gathered):
        dkv, dq = chunk_grads(keys, flat_q, flat_dout, norms, dots, dq)
        parts = lax.all_to_all(dkv.reshape(chips, rows, key_width), CHIP_AXES, 0, 0, tiled=True)
        latent_parts.append(jnp.sum(parts.astype(jnp.float32), axis=0))
    latent_grad = jnp.concatenate(latent_parts, axis=0)
    count = half * heads
    returned = lax.ppermute(dq[count:], "core", [(0, 1), (1, 0)])
    query_grad = ((dq[:count] + returned) * softmax_scale).reshape(half, heads, key_width)
    return (query_grad, latent_grad)


def solution(mesh):
    fine = Mesh(mesh.devices.reshape(4, 2, 4, 2, 2), FINE_AXES)
    query, head = ("x", "y_lo"), ("z", "core")
    in_specs = (
        P(query, head, None),
        P(FINE_AXES, None),
        P(query, head, None),
        P(query, head),
        P(query, head),
    )
    out_specs = (P(query + ("y_hi",), head, None), P(FINE_AXES, None))
    return jax.shard_map(on_device, mesh=fine, in_specs=in_specs, out_specs=out_specs, check_vma=False)
```

```python
import functools
import math

import jax
import jax.numpy as jnp
from jax import lax
from jax.experimental import pallas as pl
from jax.experimental.pallas import tpu as pltpu
from jax.sharding import Mesh, PartitionSpec as P

softmax_scale = 192.0 ** (-0.5) * (0.1 * math.log(40.0) + 1.0) ** 2
log2_e = math.log2(math.e)

FINE_AXES = ("z", "core", "x", "y_lo", "y_hi")
CHIPS = ("z", "x", "y_lo")
PLANE = ("z", "x")
TILE = 512

NT = (((1,), (1,)), ((), ()))
NN = (((1,), (0,)), ((), ()))
TN = (((0,), (0,)), ((), ()))
VMEM = pl.BlockSpec(memory_space=pltpu.VMEM)
HBM = pl.BlockSpec(memory_space=pl.ANY)


def f32_dot(left, right, dims):
    return lax.dot_general(left, right, dims, preferred_element_type=jnp.float32)


def in_vmem(array):
    return pltpu.with_memory_space_constraint(array, pltpu.VMEM)


def in_hbm(array):
    return pltpu.with_memory_space_constraint(array, pltpu.HBM)


def swap(array, axis):
    return lax.ppermute(array, axis, [(0, 1), (1, 0)])


def grads_kernel(first, last, n_before, *refs):
    refs = list(refs)
    take = lambda number: [refs.pop(0) for _ in range(number)]
    _, key_ref, q_ref, do_ref, stat_ref = take(5)
    sum_in = [] if first else take(2)
    take(n_before)
    dq_ref = refs.pop(0)
    dkv_ref = refs.pop(0) if last else None
    key_acc, value_acc = refs
    step = pl.program_id(0)
    rows, width = value_acc.shape
    key_width = key_ref.shape[-1]

    @pl.when(step == 0)
    def _():
        key_acc[...] = jnp.zeros_like(key_acc) if first else sum_in[0][...]
        value_acc[...] = jnp.zeros_like(value_acc) if first else sum_in[1][...]

    keys = key_ref[...].reshape(rows, key_width)
    queries = q_ref[...]
    douts = do_ref[...]
    scores = f32_dot(keys, queries, NT)
    dprobs = f32_dot(keys[:, :width], douts, NT)
    probs = jnp.exp2(scores * (softmax_scale * log2_e) - stat_ref[0:1, :] * log2_e)
    dscores = (probs * (dprobs - stat_ref[1:2, :])).astype(jnp.bfloat16)
    dq = f32_dot(dscores, keys, TN)
    if dq_ref.shape[0] == dq.shape[0]:
        dq_ref[...] = dq
    else:
        dq_ref[pl.ds(pl.multiple_of(step * TILE, TILE), TILE), :] = dq
    key_acc[...] += f32_dot(dscores, queries, NN)
    value_acc[...] += f32_dot(probs.astype(jnp.bfloat16), douts, NN)

    if last:

        @pl.when(step == pl.num_programs(0) - 1)
        def _():
            shape = dkv_ref.shape[:2]
            summed = key_acc[:, :width] * softmax_scale + value_acc[...]
            dkv_ref[:, :, :width] = summed.astype(dkv_ref.dtype).reshape(shape + (width,))
            rest = key_acc[:, width:] * softmax_scale
            dkv_ref[:, :, width:] = rest.astype(dkv_ref.dtype).reshape(shape + (key_width - width,))


def grads(keys, half, side, sums=None, last=False, stays=False, before=()):
    shards, shard, key_width = keys.shape
    rows = shards * shard
    total, width = side[1].shape
    count = total // 2
    tiles = count // TILE
    first = sums is None
    tile = lambda columns: pl.BlockSpec((TILE, columns), lambda i, at: (at[0] * tiles + i, 0))
    operands = [half, in_vmem(keys)] + [in_hbm(array) for array in side]
    in_specs = [VMEM, tile(key_width), tile(width), pl.BlockSpec((2, TILE), lambda i, at: (0, at[0] * tiles + i))]
    sum_shapes = [(rows, key_width), (rows, width)]
    out_shape = [(pltpu.VMEM if stays else pltpu.HBM)((count, key_width), jnp.float32)]
    out_specs = [VMEM if stays else pl.BlockSpec((TILE, key_width), lambda i, at: (i, 0))]
    aliases, scratch = {}, []
    if last:
        out_shape.append(pltpu.HBM(keys.shape, keys.dtype))
        out_specs.append(pl.BlockSpec(keys.shape, lambda i, at: (0, 0, 0)))
        scratch = [pltpu.VMEM(shape, jnp.float32) for shape in sum_shapes]
    else:
        out_shape += [pltpu.VMEM(shape, jnp.float32) for shape in sum_shapes]
        out_specs += [VMEM, VMEM]
    if not first:
        if not last:
            aliases = {len(operands): 1, len(operands) + 1: 2}
        operands += [in_vmem(array) for array in sums]
        in_specs += [VMEM, VMEM]
    operands += before
    in_specs += [HBM] * len(before)
    return pl.pallas_call(
        functools.partial(grads_kernel, first, last, len(before)),
        grid_spec=pltpu.PrefetchScalarGridSpec(
            num_scalar_prefetch=1, grid=(tiles,), in_specs=in_specs, out_specs=out_specs, scratch_shapes=scratch
        ),
        out_shape=out_shape,
        input_output_aliases=aliases,
        compiler_params=pltpu.CompilerParams(vmem_limit_bytes=30 << 20),
        cost_estimate=pl.CostEstimate(
            flops=2 * rows * count * (3 * key_width + 2 * width),
            bytes_accessed=count * (key_width * 6 + width * 2) + rows * key_width * 4,
            transcendentals=rows * count,
        ),
        name="grads",
    )(*operands)


def add_kernel(out_scale, *refs):
    *addends, out_ref = refs
    rows = out_ref.shape[0]
    at = pl.ds(pl.program_id(0) * rows, rows)
    total = addends[0][at].astype(jnp.float32)
    for addend in addends[1:]:
        total += addend[at].astype(jnp.float32)
    out_ref[...] = (total * out_scale if out_scale else total).astype(out_ref.dtype)


def add(addends, dtype, out_scale=None):
    rows, heads, key_width = addends[0].shape
    steps = 4
    return pl.pallas_call(
        functools.partial(add_kernel, out_scale),
        grid=(steps,),
        in_specs=[VMEM] * len(addends),
        out_specs=pl.BlockSpec((rows // steps, heads, key_width), lambda i: (i, 0, 0)),
        out_shape=pltpu.HBM((rows, heads, key_width), dtype),
        compiler_params=pltpu.CompilerParams(vmem_limit_bytes=12 << 20),
        cost_estimate=pl.CostEstimate(
            flops=rows * heads * key_width * 2, bytes_accessed=rows * heads * key_width * 4, transcendentals=0
        ),
        name="add",
    )(*[in_vmem(addend) for addend in addends])


def sum_kernel(place, parts_ref, after_ref, mine_ref, other_ref):
    shard = mine_ref.shape[0]
    for out_ref, at in ((mine_ref, place[0]), (other_ref, 1 - place[0])):
        rows = pl.ds(pl.multiple_of(at * shard, shard), shard)
        total = parts_ref[0, rows, :].astype(jnp.float32)
        for part in range(1, parts_ref.shape[0]):
            total += parts_ref[part, rows, :].astype(jnp.float32)
        out_ref[...] = total


def sum_parts(parts, place, after):
    _, rows, key_width = parts.shape
    return pl.pallas_call(
        sum_kernel,
        grid_spec=pltpu.PrefetchScalarGridSpec(
            num_scalar_prefetch=1, grid=(1,), in_specs=[VMEM, HBM], out_specs=[VMEM, VMEM]
        ),
        out_shape=[jax.ShapeDtypeStruct((rows // 2, key_width), jnp.float32)] * 2,
        name="sum_parts",
    )(place, in_vmem(parts), after)


def on_device(queries, latent, out_grad, log_norms, row_dots):
    number, heads, key_width = queries.shape
    shard = latent.shape[0]
    half = number // 2

    spread = jnp.broadcast_to(latent[None], (lax.axis_size(CHIPS), shard, key_width))
    keys = lax.all_to_all(spread, CHIPS, 0, 0, tiled=True)

    def flat(queries, out_grad, stats):
        rows = number * heads
        return (
            queries.reshape(rows, key_width),
            out_grad.reshape(rows, out_grad.shape[2]),
            stats.reshape(2, rows),
        )

    mine = (queries, out_grad, jnp.stack([log_norms, row_dots]))
    theirs = flat(*[swap(array, "core") for array in mine])
    mine = flat(*mine)

    kept = lax.axis_index("y_hi").astype(jnp.int32)[None]
    sent = 1 - kept
    whole = (half, heads, key_width)
    dq_sent_theirs, *sums = grads(keys, sent, theirs, before=mine)
    dq_sent_mine, *sums = grads(keys, sent, mine, sums=sums, stays=True)
    returned = swap(dq_sent_theirs.reshape(whole), "core")
    over_cores = add([dq_sent_mine.reshape(whole), returned], jnp.bfloat16)
    received = swap(over_cores, "y_hi")
    dq_theirs, *sums = grads(keys, kept, theirs, sums=sums, before=[over_cores])
    dq_mine, dkv = grads(keys, kept, mine, sums=sums, last=True, stays=True)
    returned = swap(dq_theirs.reshape(whole), "core")
    query_grad = add([dq_mine.reshape(whole), returned, received], jnp.float32, softmax_scale)
    parts = lax.all_to_all(dkv.reshape(-1, 2 * shard, key_width), PLANE, 0, 0, tiled=True)
    own, other = sum_parts(parts, lax.axis_index("y_lo").astype(jnp.int32)[None], query_grad)
    return (query_grad, own + swap(other, "y_lo"))


def solution(mesh):
    fine = Mesh(mesh.devices.reshape(4, 2, 4, 2, 2), FINE_AXES)
    query, head = ("x", "y_lo"), ("z", "core")
    in_specs = (
        P(query, head, None),
        P(FINE_AXES, None),
        P(query, head, None),
        P(query, head),
        P(query, head),
    )
    out_specs = (P(query + ("y_hi",), head, None), P(FINE_AXES, None))
    return jax.shard_map(on_device, mesh=fine, in_specs=in_specs, out_specs=out_specs, check_vma=False)
```

```python
import functools
import math

import jax
import jax.numpy as jnp
from jax import lax
from jax.experimental import pallas as pl
from jax.experimental.pallas import tpu as pltpu
from jax.sharding import Mesh, PartitionSpec as P

softmax_scale = 192.0 ** (-0.5) * (0.1 * math.log(40.0) + 1.0) ** 2
log2_e = math.log2(math.e)

FINE_AXES = ("z", "core", "x", "y_lo", "y_hi")
CHIPS = ("z", "x", "y_lo")
PLANE = ("z", "x")
TILE = 512

NT = (((1,), (1,)), ((), ()))
NN = (((1,), (0,)), ((), ()))
TN = (((0,), (0,)), ((), ()))
VMEM = pl.BlockSpec(memory_space=pltpu.VMEM)
HBM = pl.BlockSpec(memory_space=pl.ANY)


def f32_dot(left, right, dims):
    return lax.dot_general(left, right, dims, preferred_element_type=jnp.float32)


def in_vmem(array):
    return pltpu.with_memory_space_constraint(array, pltpu.VMEM)


def in_hbm(array):
    return pltpu.with_memory_space_constraint(array, pltpu.HBM)


def swap(array, axis):
    return lax.ppermute(array, axis, [(0, 1), (1, 0)])


def grads_kernel(first, last, stays, do_stays, n_halves, n_before, *refs):
    refs = list(refs)
    take = lambda number: [refs.pop(0) for _ in range(number)]
    half, key_ref, q_hbm, do_hbm, stat_ref = take(5)
    sum_in = [] if first else take(2)
    take(n_before)
    dq_refs = take(n_halves)
    dkv_ref = refs.pop(0) if last else None
    key_acc, value_acc, q_tiles, sems, *refs = refs
    dq_tiles = [] if stays else [refs.pop(0)]
    do_tiles = refs
    rows, width = value_acc.shape
    key_width = key_ref.shape[-1]
    count = dq_refs[0].shape[0]
    per_half = count // TILE

    def begin(tile):
        side = half[0] if tile < per_half else 1 - half[0]
        return pl.multiple_of(side * count, TILE) + tile % per_half * TILE

    copies, results = [], []
    for tile in range(n_halves * per_half):
        at = pl.ds(begin(tile), TILE)
        pair = [pltpu.make_async_copy(q_hbm.at[at, :], q_tiles.at[tile], sems.at[0, tile])]
        if not do_stays:
            pair.append(pltpu.make_async_copy(do_hbm.at[at, :], do_tiles[0].at[tile], sems.at[1, tile]))
        for copy in pair:
            copy.start()
        copies.append(pair)

    keys = key_ref[...].reshape(rows, key_width)
    for tile, pair in enumerate(copies):
        for copy in pair:
            copy.wait()
        queries = q_tiles[tile]
        douts = do_hbm[pl.ds(begin(tile), TILE), :] if do_stays else do_tiles[0][tile]
        side = half[0] if tile < per_half else 1 - half[0]
        stats = stat_ref[side * per_half + tile % per_half]
        scores = f32_dot(keys, queries, NT)
        dprobs = f32_dot(keys[:, :width], douts, NT)
        probs = jnp.exp2(scores * (softmax_scale * log2_e) - stats[0:1, :] * log2_e)
        dscores = (probs * (dprobs - stats[1:2, :])).astype(jnp.bfloat16)
        dq_at = dq_refs[tile // per_half].at[pl.ds(tile % per_half * TILE, TILE), :]
        if stays:
            dq_at[...] = f32_dot(dscores, keys, TN)
        else:
            dq_tiles[0][tile] = f32_dot(dscores, keys, TN)
            result = pltpu.make_async_copy(dq_tiles[0].at[tile], dq_at, sems.at[2, tile])
            result.start()
            results.append(result)
        key_part = f32_dot(dscores, queries, NN)
        value_part = f32_dot(probs.astype(jnp.bfloat16), douts, NN)
        if tile > 0:
            key_acc[...] += key_part
            value_acc[...] += value_part
        elif first:
            key_acc[...] = key_part
            value_acc[...] = value_part
        else:
            key_acc[...] = sum_in[0][...] + key_part
            value_acc[...] = sum_in[1][...] + value_part

    if last:
        shape = dkv_ref.shape[:2]
        summed = key_acc[:, :width] * softmax_scale + value_acc[...]
        dkv_ref[:, :, :width] = summed.astype(dkv_ref.dtype).reshape(shape + (width,))
        rest = key_acc[:, width:] * softmax_scale
        dkv_ref[:, :, width:] = rest.astype(dkv_ref.dtype).reshape(shape + (key_width - width,))
    for result in results:
        result.wait()


def grads(keys, half, side, halves=1, sums=None, last=False, stays=False, do_stays=False, before=()):
    shards, shard, key_width = keys.shape
    rows = shards * shard
    queries, douts, stats = side
    total, width = douts.shape
    count = total // 2
    tiles = halves * count // TILE
    first = sums is None
    operands = [half, in_vmem(keys), in_hbm(queries), (in_vmem if do_stays else in_hbm)(douts), in_vmem(stats)]
    in_specs = [VMEM, HBM, VMEM if do_stays else HBM, VMEM]
    sum_shapes = [(rows, key_width), (rows, width)]
    out_shape = [(pltpu.VMEM if stays else pltpu.HBM)((count, key_width), jnp.float32)] * halves
    out_specs = [VMEM if stays else HBM] * halves
    scratch = [
        pltpu.VMEM((tiles, TILE, key_width), queries.dtype),
        pltpu.SemaphoreType.DMA((3, tiles)),
    ]
    if not stays:
        scratch.append(pltpu.VMEM((tiles, TILE, key_width), jnp.float32))
    if not do_stays:
        scratch.append(pltpu.VMEM((tiles, TILE, width), douts.dtype))
    aliases = {}
    if not first:
        if not last:
            aliases = {len(operands): halves, len(operands) + 1: halves + 1}
        operands += [in_vmem(array) for array in sums]
        in_specs += [VMEM, VMEM]
    if last:
        out_shape.append(pltpu.HBM(keys.shape, keys.dtype))
        out_specs.append(pl.BlockSpec(keys.shape, lambda i, at: (0, 0, 0)))
        scratch = [pltpu.VMEM(shape, jnp.float32) for shape in sum_shapes] + scratch
    else:
        out_shape += [pltpu.VMEM(shape, jnp.float32) for shape in sum_shapes]
        out_specs += [VMEM, VMEM]
    operands += [in_hbm(array) for array in before]
    in_specs += [HBM] * len(before)
    return pl.pallas_call(
        functools.partial(grads_kernel, first, last, stays, do_stays, halves, len(before)),
        grid_spec=pltpu.PrefetchScalarGridSpec(
            num_scalar_prefetch=1, grid=(1,), in_specs=in_specs, out_specs=out_specs, scratch_shapes=scratch
        ),
        out_shape=out_shape,
        input_output_aliases=aliases,
        compiler_params=pltpu.CompilerParams(vmem_limit_bytes=32 << 20),
        cost_estimate=pl.CostEstimate(flops=rows * count, bytes_accessed=rows * key_width * 2, transcendentals=rows),
        name="grads",
    )(*operands)


def add_kernel(out_scale, *refs):
    *addends, out_ref = refs
    rows = out_ref.shape[0]
    at = pl.ds(pl.program_id(0) * rows, rows)
    parts = [addend[...] if addend.shape[0] == rows else addend[at] for addend in addends]
    total = parts[0].astype(jnp.float32)
    for part in parts[1:]:
        total += part.astype(jnp.float32)
    out_ref[...] = (total * out_scale if out_scale else total).astype(out_ref.dtype)


def add(addends, dtype, out_scale=None, resident=True):
    rows, heads, key_width = addends[0].shape
    steps = 4
    block = pl.BlockSpec((rows // steps, heads, key_width), lambda i: (i, 0, 0))
    return pl.pallas_call(
        functools.partial(add_kernel, out_scale),
        grid=(steps,),
        in_specs=[VMEM if resident else block] * len(addends),
        out_specs=block,
        out_shape=pltpu.HBM((rows, heads, key_width), dtype),
        compiler_params=pltpu.CompilerParams(vmem_limit_bytes=12 << 20),
        cost_estimate=pl.CostEstimate(
            flops=rows * heads * key_width * 2, bytes_accessed=rows * heads * key_width * 4, transcendentals=0
        ),
        name="add",
    )(*[(in_vmem if resident else in_hbm)(addend) for addend in addends])


def sum_kernel(place, parts_ref, after_ref, mine_ref, other_ref):
    shard = mine_ref.shape[0]
    for out_ref, at in ((mine_ref, place[0]), (other_ref, 1 - place[0])):
        rows = pl.ds(pl.multiple_of(at * shard, shard), shard)
        total = parts_ref[0, rows, :].astype(jnp.float32)
        for part in range(1, parts_ref.shape[0]):
            total += parts_ref[part, rows, :].astype(jnp.float32)
        out_ref[...] = total


def sum_parts(parts, place, after):
    _, rows, key_width = parts.shape
    return pl.pallas_call(
        sum_kernel,
        grid_spec=pltpu.PrefetchScalarGridSpec(
            num_scalar_prefetch=1, grid=(1,), in_specs=[VMEM, HBM], out_specs=[VMEM, VMEM]
        ),
        out_shape=[jax.ShapeDtypeStruct((rows // 2, key_width), jnp.float32)] * 2,
        compiler_params=pltpu.CompilerParams(vmem_limit_bytes=4 << 20),
        name="sum_parts",
    )(place, in_vmem(parts), in_hbm(after))


def on_device(queries, latent, out_grad, log_norms, row_dots):
    number, heads, key_width = queries.shape
    shard = latent.shape[0]
    half = number // 2

    spread = jnp.broadcast_to(latent[None], (lax.axis_size(CHIPS), shard, key_width))
    keys = lax.all_to_all(spread, CHIPS, 0, 0, tiled=True)

    def flat(queries, out_grad, stats):
        rows = number * heads
        return (
            queries.reshape(rows, key_width),
            out_grad.reshape(rows, out_grad.shape[2]),
            stats.reshape(2, rows // TILE, TILE).transpose(1, 0, 2),
        )

    mine = (queries, out_grad, jnp.stack([log_norms, row_dots]))
    theirs = flat(*[swap(array, "core") for array in mine])
    mine = flat(*mine)

    kept = lax.axis_index("y_hi").astype(jnp.int32)[None]
    sent = 1 - kept
    whole = (half, heads, key_width)
    dq_sent_theirs, dq_theirs, *sums = grads(keys, sent, theirs, halves=2, do_stays=True, before=mine)
    returned = swap(dq_sent_theirs.reshape(whole), "core")
    dq_sent_mine, *sums = grads(keys, sent, mine, sums=sums, stays=True)
    over_cores = add([dq_sent_mine.reshape(whole), returned], jnp.bfloat16)
    received = swap(over_cores, "y_hi")
    dq_mine, dkv = grads(keys, kept, mine, sums=sums, last=True, before=[over_cores])
    returned = swap(dq_theirs.reshape(whole), "core")
    query_grad = add([dq_mine.reshape(whole), returned, received], jnp.float32, softmax_scale, resident=False)
    parts = lax.all_to_all(dkv.reshape(-1, 2 * shard, key_width), PLANE, 0, 0, tiled=True)
    own, other = sum_parts(parts, lax.axis_index("y_lo").astype(jnp.int32)[None], query_grad)
    return (query_grad, own + swap(other, "y_lo"))


def solution(mesh):
    fine = Mesh(mesh.devices.reshape(4, 2, 4, 2, 2), FINE_AXES)
    query, head = ("x", "y_lo"), ("z", "core")
    in_specs = (
        P(query, head, None),
        P(FINE_AXES, None),
        P(query, head, None),
        P(query, head),
        P(query, head),
    )
    out_specs = (P(query + ("y_hi",), head, None), P(FINE_AXES, None))
    return jax.shard_map(on_device, mesh=fine, in_specs=in_specs, out_specs=out_specs, check_vma=False)
```

```python
import functools
import math

import jax
import jax.numpy as jnp
from jax import lax
from jax.experimental import pallas as pl
from jax.experimental.pallas import tpu as pltpu
from jax.sharding import Mesh, PartitionSpec as P

softmax_scale = 192.0 ** (-0.5) * (0.1 * math.log(40.0) + 1.0) ** 2
log2_e = math.log2(math.e)

FINE_AXES = ("z", "core", "x", "y_lo", "y_hi")
CHIPS = ("z", "x", "y_lo")
PLANE = ("z", "x")
TILE = 512

NT = (((1,), (1,)), ((), ()))
NN = (((1,), (0,)), ((), ()))
VMEM = pl.BlockSpec(memory_space=pltpu.VMEM)
HBM = pl.BlockSpec(memory_space=pl.ANY)


def f32_dot(left, right, dims):
    return lax.dot_general(left, right, dims, preferred_element_type=jnp.float32)


def in_vmem(array):
    return pltpu.with_memory_space_constraint(array, pltpu.VMEM)


def in_hbm(array):
    return pltpu.with_memory_space_constraint(array, pltpu.HBM)


def swap(array, axis):
    return lax.ppermute(array, axis, [(0, 1), (1, 0)])


def grads_kernel(first, last, stays, do_stays, n_halves, n_before, *refs):
    refs = list(refs)
    take = lambda number: [refs.pop(0) for _ in range(number)]
    half, key_ref, q_hbm, do_hbm, stat_ref = take(5)
    sum_in = [] if first else take(2)
    take(n_before)
    dq_refs = take(n_halves)
    dkv_ref = refs.pop(0) if last else None
    key_acc, value_acc, q_tiles, sems, *refs = refs
    dq_tiles = [] if stays else [refs.pop(0)]
    do_tiles = refs
    rows, width = value_acc.shape
    key_width = key_ref.shape[-1]
    count = dq_refs[0].shape[0]
    per_half = count // TILE

    def begin(tile):
        side = half[0] if tile < per_half else 1 - half[0]
        return pl.multiple_of(side * count, TILE) + tile % per_half * TILE

    copies, results = [], []
    for tile in range(n_halves * per_half):
        at = pl.ds(begin(tile), TILE)
        pair = [pltpu.make_async_copy(q_hbm.at[at, :], q_tiles.at[tile], sems.at[0, tile])]
        if not do_stays:
            pair.append(pltpu.make_async_copy(do_hbm.at[at, :], do_tiles[0].at[tile], sems.at[1, tile]))
        for copy in pair:
            copy.start()
        copies.append(pair)

    keys = key_ref[...].reshape(rows, key_width)
    keys_t = keys.T
    for tile, pair in enumerate(copies):
        for copy in pair:
            copy.wait()
        queries = q_tiles[tile]
        douts = do_hbm[pl.ds(begin(tile), TILE), :] if do_stays else do_tiles[0][tile]
        side = half[0] if tile < per_half else 1 - half[0]
        stats = stat_ref[side * per_half + tile % per_half]
        scores = f32_dot(keys, queries, NT)
        dprobs = f32_dot(keys[:, :width], douts, NT)
        probs = jnp.exp2(scores * (softmax_scale * log2_e) - stats[0:1, :] * log2_e)
        dscores = (probs * (dprobs - stats[1:2, :])).astype(jnp.bfloat16)
        dq_at = dq_refs[tile // per_half].at[pl.ds(tile % per_half * TILE, TILE), :]
        if stays:
            dq_at[...] = f32_dot(keys_t, dscores, NN).T
        else:
            dq_tiles[0][tile] = f32_dot(keys_t, dscores, NN).T
            result = pltpu.make_async_copy(dq_tiles[0].at[tile], dq_at, sems.at[2, tile])
            result.start()
            results.append(result)
        key_part = f32_dot(queries.T, dscores, NT)
        value_part = f32_dot(probs.astype(jnp.bfloat16), douts, NN)
        if tile > 0:
            key_acc[...] += key_part
            value_acc[...] += value_part
        elif first:
            key_acc[...] = key_part
            value_acc[...] = value_part
        else:
            key_acc[...] = sum_in[0][...] + key_part
            value_acc[...] = sum_in[1][...] + value_part

    if last:
        shape = dkv_ref.shape[:2]
        key_sum = key_acc[...].T * softmax_scale
        summed = key_sum[:, :width] + value_acc[...]
        dkv_ref[:, :, :width] = summed.astype(dkv_ref.dtype).reshape(shape + (width,))
        rest = key_sum[:, width:]
        dkv_ref[:, :, width:] = rest.astype(dkv_ref.dtype).reshape(shape + (key_width - width,))
    for result in results:
        result.wait()


def grads(keys, half, side, halves=1, sums=None, last=False, stays=False, do_stays=False, before=()):
    shards, shard, key_width = keys.shape
    rows = shards * shard
    queries, douts, stats = side
    total, width = douts.shape
    count = total // 2
    tiles = halves * count // TILE
    first = sums is None
    operands = [half, in_vmem(keys), in_hbm(queries), (in_vmem if do_stays else in_hbm)(douts), in_vmem(stats)]
    in_specs = [VMEM, HBM, VMEM if do_stays else HBM, VMEM]
    sum_shapes = [(key_width, rows), (rows, width)]
    out_shape = [(pltpu.VMEM if stays else pltpu.HBM)((count, key_width), jnp.float32)] * halves
    out_specs = [VMEM if stays else HBM] * halves
    scratch = [
        pltpu.VMEM((tiles, TILE, key_width), queries.dtype),
        pltpu.SemaphoreType.DMA((3, tiles)),
    ]
    if not stays:
        scratch.append(pltpu.VMEM((tiles, TILE, key_width), jnp.float32))
    if not do_stays:
        scratch.append(pltpu.VMEM((tiles, TILE, width), douts.dtype))
    aliases = {}
    if not first:
        if not last:
            aliases = {len(operands): halves, len(operands) + 1: halves + 1}
        operands += [in_vmem(array) for array in sums]
        in_specs += [VMEM, VMEM]
    if last:
        out_shape.append(pltpu.HBM(keys.shape, keys.dtype))
        out_specs.append(pl.BlockSpec(keys.shape, lambda i, at: (0, 0, 0)))
        scratch = [pltpu.VMEM(shape, jnp.float32) for shape in sum_shapes] + scratch
    else:
        out_shape += [pltpu.VMEM(shape, jnp.float32) for shape in sum_shapes]
        out_specs += [VMEM, VMEM]
    operands += [in_hbm(array) for array in before]
    in_specs += [HBM] * len(before)
    return pl.pallas_call(
        functools.partial(grads_kernel, first, last, stays, do_stays, halves, len(before)),
        grid_spec=pltpu.PrefetchScalarGridSpec(
            num_scalar_prefetch=1, grid=(1,), in_specs=in_specs, out_specs=out_specs, scratch_shapes=scratch
        ),
        out_shape=out_shape,
        input_output_aliases=aliases,
        compiler_params=pltpu.CompilerParams(vmem_limit_bytes=32 << 20),
        cost_estimate=pl.CostEstimate(flops=rows * count, bytes_accessed=rows * key_width * 2, transcendentals=rows),
        name="grads",
    )(*operands)


def add_kernel(out_scale, *refs):
    *addends, out_ref = refs
    rows = out_ref.shape[0]
    at = pl.ds(pl.program_id(0) * rows, rows)
    parts = [addend[...] if addend.shape[0] == rows else addend[at] for addend in addends]
    total = parts[0].astype(jnp.float32)
    for part in parts[1:]:
        total += part.astype(jnp.float32)
    out_ref[...] = (total * out_scale if out_scale else total).astype(out_ref.dtype)


def add(addends, dtype, out_scale=None, resident=None):
    rows, heads, key_width = addends[0].shape
    steps = 4
    resident = resident or [True] * len(addends)
    block = pl.BlockSpec((rows // steps, heads, key_width), lambda i: (i, 0, 0))
    return pl.pallas_call(
        functools.partial(add_kernel, out_scale),
        grid=(steps,),
        in_specs=[VMEM if stays else block for stays in resident],
        out_specs=block,
        out_shape=pltpu.HBM((rows, heads, key_width), dtype),
        compiler_params=pltpu.CompilerParams(vmem_limit_bytes=12 << 20),
        cost_estimate=pl.CostEstimate(
            flops=rows * heads * key_width * 2, bytes_accessed=rows * heads * key_width * 4, transcendentals=0
        ),
        name="add",
    )(*[(in_vmem if stays else in_hbm)(addend) for addend, stays in zip(addends, resident)])


def sum_kernel(place, parts_ref, mine_ref, other_ref):
    shard = mine_ref.shape[0]
    for out_ref, at in ((mine_ref, place[0]), (other_ref, 1 - place[0])):
        rows = pl.ds(pl.multiple_of(at * shard, shard), shard)
        total = parts_ref[0, rows, :].astype(jnp.float32)
        for part in range(1, parts_ref.shape[0]):
            total += parts_ref[part, rows, :].astype(jnp.float32)
        out_ref[...] = total


def sum_parts(parts, place):
    _, rows, key_width = parts.shape
    return pl.pallas_call(
        sum_kernel,
        grid_spec=pltpu.PrefetchScalarGridSpec(num_scalar_prefetch=1, grid=(1,), in_specs=[VMEM], out_specs=[VMEM, VMEM]),
        out_shape=[pltpu.VMEM((rows // 2, key_width), jnp.float32)] * 2,
        compiler_params=pltpu.CompilerParams(vmem_limit_bytes=4 << 20),
        name="sum_parts",
    )(place, in_vmem(parts))


def join_kernel(own_ref, other_ref, after_ref, out_ref):
    out_ref[...] = own_ref[...] + other_ref[...]


def join(own, other, after):
    return pl.pallas_call(
        join_kernel,
        in_specs=[VMEM, VMEM, HBM],
        out_specs=VMEM,
        out_shape=jax.ShapeDtypeStruct(own.shape, own.dtype),
        compiler_params=pltpu.CompilerParams(vmem_limit_bytes=4 << 20),
        name="join",
    )(in_vmem(own), in_vmem(other), in_hbm(after))


def on_device(queries, latent, out_grad, log_norms, row_dots):
    number, heads, key_width = queries.shape
    shard = latent.shape[0]
    half = number // 2

    spread = jnp.broadcast_to(latent[None], (lax.axis_size(CHIPS), shard, key_width))
    keys = lax.all_to_all(spread, CHIPS, 0, 0, tiled=True)

    def flat(queries, out_grad, stats):
        rows = number * heads
        return (
            queries.reshape(rows, key_width),
            out_grad.reshape(rows, out_grad.shape[2]),
            stats.reshape(2, rows // TILE, TILE).transpose(1, 0, 2),
        )

    mine = (queries, out_grad, jnp.stack([log_norms, row_dots]))
    theirs = flat(*[swap(array, "core") for array in mine])
    mine = flat(*mine)

    kept = lax.axis_index("y_hi").astype(jnp.int32)[None]
    sent = 1 - kept
    whole = (half, heads, key_width)
    dq_sent_theirs, dq_theirs, *sums = grads(keys, sent, theirs, halves=2, do_stays=True, before=mine)
    returned = swap(dq_sent_theirs.reshape(whole), "core")
    dq_sent_mine, *sums = grads(keys, sent, mine, sums=sums, stays=True)
    over_cores = add([dq_sent_mine.reshape(whole), returned], jnp.bfloat16)
    received = swap(over_cores, "y_hi")
    dq_mine, dkv = grads(keys, kept, mine, sums=sums, last=True, before=[over_cores])
    returned = swap(dq_theirs.reshape(whole), "core")
    query_grad = add([dq_mine.reshape(whole), returned, received], jnp.float32, softmax_scale, resident=[False, False, True])
    parts = lax.all_to_all(dkv.reshape(-1, 2 * shard, key_width), PLANE, 0, 0, tiled=True)
    own, other = sum_parts(parts, lax.axis_index("y_lo").astype(jnp.int32)[None])
    return (query_grad, join(own, swap(other, "y_lo"), query_grad))


def solution(mesh):
    fine = Mesh(mesh.devices.reshape(4, 2, 4, 2, 2), FINE_AXES)
    query, head = ("x", "y_lo"), ("z", "core")
    in_specs = (
        P(query, head, None),
        P(FINE_AXES, None),
        P(query, head, None),
        P(query, head),
        P(query, head),
    )
    out_specs = (P(query + ("y_hi",), head, None), P(FINE_AXES, None))
    return jax.shard_map(on_device, mesh=fine, in_specs=in_specs, out_specs=out_specs, check_vma=False)
```

```python
import functools
import math

import jax
import jax.numpy as jnp
from jax import lax
from jax.experimental import pallas as pl
from jax.experimental.pallas import tpu as pltpu
from jax.sharding import Mesh, PartitionSpec as P

softmax_scale = 192.0 ** (-0.5) * (0.1 * math.log(40.0) + 1.0) ** 2
log2_e = math.log2(math.e)

FINE_AXES = ("z", "core", "x", "y_lo", "y_hi")
CHIPS = ("z", "x", "y_lo")
PLANE = ("z", "x")
TILE = 512
PIECES = 4

NT = (((1,), (1,)), ((), ()))
NN = (((1,), (0,)), ((), ()))
VMEM = pl.BlockSpec(memory_space=pltpu.VMEM)
HBM = pl.BlockSpec(memory_space=pl.ANY)


def f32_dot(left, right, dims):
    return lax.dot_general(left, right, dims, preferred_element_type=jnp.float32)


def in_vmem(array):
    return pltpu.with_memory_space_constraint(array, pltpu.VMEM)


def in_hbm(array):
    return pltpu.with_memory_space_constraint(array, pltpu.HBM)


def core_sum_kernel(mine_ref, theirs_ref, out_ref):
    out_ref[...] = (mine_ref[...] + theirs_ref[...]).astype(out_ref.dtype)


def core_sum(mine, theirs):
    return pl.pallas_call(
        core_sum_kernel,
        in_specs=[VMEM, VMEM],
        out_specs=VMEM,
        out_shape=pltpu.VMEM(mine.shape, jnp.bfloat16),
        compiler_params=pltpu.CompilerParams(vmem_limit_bytes=4 << 20),
        cost_estimate=pl.CostEstimate(flops=mine.size, bytes_accessed=mine.size, transcendentals=0),
        name="core_sum",
    )(in_vmem(mine), in_vmem(theirs))


def swap(array, axis):
    return lax.ppermute(array, axis, [(0, 1), (1, 0)])


def grads_kernel(first, last, stays, do_stays, n_halves, n_before, *refs):
    refs = list(refs)
    take = lambda number: [refs.pop(0) for _ in range(number)]
    half, key_ref, q_hbm, do_hbm, stat_ref = take(5)
    sum_in = [] if first else take(2)
    take(n_before)
    dq_refs = take(n_halves)
    dkv_ref = refs.pop(0) if last else None
    key_acc, value_acc, q_tiles, sems, *refs = refs
    dkv_tiles = refs.pop() if last else None
    dq_tiles = [] if stays else [refs.pop(0)]
    do_tiles = refs
    rows, width = value_acc.shape
    key_width = key_ref.shape[-1]
    count = dq_refs[0].shape[0]
    per_half = count // TILE

    def begin(tile):
        side = half[0] if tile < per_half else 1 - half[0]
        return pl.multiple_of(side * count, TILE) + tile % per_half * TILE

    copies, results = [], []
    for tile in range(n_halves * per_half):
        at = pl.ds(begin(tile), TILE)
        pair = [pltpu.make_async_copy(q_hbm.at[at, :], q_tiles.at[tile], sems.at[0, tile])]
        if not do_stays:
            pair.append(pltpu.make_async_copy(do_hbm.at[at, :], do_tiles[0].at[tile], sems.at[1, tile]))
        for copy in pair:
            copy.start()
        copies.append(pair)

    keys = key_ref[...].reshape(rows, key_width)
    keys_t = keys.T
    for tile, pair in enumerate(copies):
        for copy in pair:
            copy.wait()
        queries = q_tiles[tile]
        douts = do_hbm[pl.ds(begin(tile), TILE), :] if do_stays else do_tiles[0][tile]
        side = half[0] if tile < per_half else 1 - half[0]
        stats = stat_ref[side * per_half + tile % per_half]
        scores = f32_dot(keys, queries, NT)
        dprobs = f32_dot(keys[:, :width], douts, NT)
        probs = jnp.exp2(scores * (softmax_scale * log2_e) - stats[0:1, :] * log2_e)
        dscores = (probs * (dprobs - stats[1:2, :])).astype(jnp.bfloat16)
        dq_at = dq_refs[tile // per_half].at[pl.ds(tile % per_half * TILE, TILE), :]
        query_part = f32_dot(keys_t, dscores, NN).T
        if stays:
            dq_at[...] = query_part
        else:
            dq_tiles[0][tile] = query_part
            result = pltpu.make_async_copy(dq_tiles[0].at[tile], dq_at, sems.at[2, tile])
            result.start()
            results.append(result)
        key_part = f32_dot(queries.T, dscores, NT)
        value_part = f32_dot(probs.astype(jnp.bfloat16), douts, NN)
        if tile > 0:
            key_acc[...] += key_part
            value_acc[...] += value_part
        elif first:
            key_acc[...] = key_part
            value_acc[...] = value_part
        else:
            key_acc[...] = sum_in[0][...] + key_part
            value_acc[...] = sum_in[1][...] + value_part
        if last and tile == len(copies) - 1:
            some = dkv_tiles.shape[0] // PIECES
            for piece in range(PIECES):
                shards = pl.ds(piece * some, some)
                at = slice(piece * rows // PIECES, (piece + 1) * rows // PIECES)
                shape = (some, dkv_tiles.shape[1])
                key_sum = key_acc[:, at].T * softmax_scale
                summed = key_sum[:, :width] + value_acc[at, :]
                dkv_tiles[shards, :, :width] = summed.astype(dkv_tiles.dtype).reshape(shape + (width,))
                rest = key_sum[:, width:].astype(dkv_tiles.dtype)
                dkv_tiles[shards, :, width:] = rest.reshape(shape + (key_width - width,))
                result = pltpu.make_async_copy(dkv_tiles.at[shards], dkv_ref.at[shards], sems.at[3, piece])
                result.start()
                results.append(result)
    for result in results:
        result.wait()


def grads(keys, half, side, halves=1, sums=None, last=False, stays=False, do_stays=False, before=()):
    shards, shard, key_width = keys.shape
    rows = shards * shard
    queries, douts, stats = side
    total, width = douts.shape
    count = total // 2
    tiles = halves * count // TILE
    first = sums is None
    operands = [half, in_vmem(keys), in_hbm(queries), (in_vmem if do_stays else in_hbm)(douts), in_vmem(stats)]
    in_specs = [VMEM, HBM, VMEM if do_stays else HBM, VMEM]
    sum_shapes = [(key_width, rows), (rows, width)]
    out_shape = [(pltpu.VMEM if stays else pltpu.HBM)((count, key_width), jnp.float32)] * halves
    out_specs = [VMEM if stays else HBM] * halves
    scratch = [
        pltpu.VMEM((tiles, TILE, key_width), queries.dtype),
        pltpu.SemaphoreType.DMA((4, max(tiles, PIECES))),
    ]
    if not stays:
        scratch.append(pltpu.VMEM((tiles, TILE, key_width), jnp.float32))
    if not do_stays:
        scratch.append(pltpu.VMEM((tiles, TILE, width), douts.dtype))
    aliases = {}
    if not first:
        if not last:
            aliases = {len(operands): halves, len(operands) + 1: halves + 1}
        operands += [in_vmem(array) for array in sums]
        in_specs += [VMEM, VMEM]
    if last:
        out_shape.append(pltpu.HBM(keys.shape, keys.dtype))
        out_specs.append(HBM)
        scratch = [pltpu.VMEM(shape, jnp.float32) for shape in sum_shapes] + scratch
        scratch.append(pltpu.VMEM(keys.shape, keys.dtype))
    else:
        out_shape += [pltpu.VMEM(shape, jnp.float32) for shape in sum_shapes]
        out_specs += [VMEM, VMEM]
    place, spec = (in_hbm, HBM) if first else (in_vmem, VMEM)
    operands += [place(array) for array in before]
    in_specs += [spec] * len(before)
    return pl.pallas_call(
        functools.partial(grads_kernel, first, last, stays, do_stays, halves, len(before)),
        grid_spec=pltpu.PrefetchScalarGridSpec(
            num_scalar_prefetch=1, grid=(1,), in_specs=in_specs, out_specs=out_specs, scratch_shapes=scratch
        ),
        out_shape=out_shape,
        input_output_aliases=aliases,
        compiler_params=pltpu.CompilerParams(vmem_limit_bytes=32 << 20),
        cost_estimate=pl.CostEstimate(flops=rows * count, bytes_accessed=rows * key_width * 2, transcendentals=rows),
        name="grads",
    )(*operands)


def add_kernel(out_scale, *refs):
    *addends, out_ref = refs
    rows = out_ref.shape[0]
    at = pl.ds(pl.program_id(0) * rows, rows)
    parts = [addend[...] if addend.shape[0] == rows else addend[at] for addend in addends]
    total = parts[0].astype(jnp.float32)
    for part in parts[1:]:
        total += part.astype(jnp.float32)
    out_ref[...] = (total * out_scale if out_scale else total).astype(out_ref.dtype)


def add(addends, dtype, out_scale=None, resident=None):
    rows, heads, key_width = addends[0].shape
    steps = 4
    resident = resident or [True] * len(addends)
    block = pl.BlockSpec((rows // steps, heads, key_width), lambda i: (i, 0, 0))
    return pl.pallas_call(
        functools.partial(add_kernel, out_scale),
        grid=(steps,),
        in_specs=[VMEM if stays else block for stays in resident],
        out_specs=block,
        out_shape=pltpu.HBM((rows, heads, key_width), dtype),
        compiler_params=pltpu.CompilerParams(vmem_limit_bytes=12 << 20),
        cost_estimate=pl.CostEstimate(
            flops=rows * heads * key_width * 2, bytes_accessed=rows * heads * key_width * 4, transcendentals=0
        ),
        name="add",
    )(*[(in_vmem if stays else in_hbm)(addend) for addend, stays in zip(addends, resident)])


def sum_kernel(place, parts_ref, mine_ref, other_ref):
    shard = mine_ref.shape[0]
    for out_ref, at in ((mine_ref, place[0]), (other_ref, 1 - place[0])):
        rows = pl.ds(pl.multiple_of(at * shard, shard), shard)
        total = parts_ref[0, rows, :].astype(jnp.float32)
        for part in range(1, parts_ref.shape[0]):
            total += parts_ref[part, rows, :].astype(jnp.float32)
        out_ref[...] = total


def sum_parts(parts, place):
    _, rows, key_width = parts.shape
    return pl.pallas_call(
        sum_kernel,
        grid_spec=pltpu.PrefetchScalarGridSpec(num_scalar_prefetch=1, grid=(1,), in_specs=[VMEM], out_specs=[VMEM, VMEM]),
        out_shape=[pltpu.VMEM((rows // 2, key_width), jnp.float32)] * 2,
        compiler_params=pltpu.CompilerParams(vmem_limit_bytes=4 << 20),
        name="sum_parts",
    )(place, in_vmem(parts))


def join_kernel(own_ref, other_ref, after_ref, out_ref):
    out_ref[...] = own_ref[...] + other_ref[...]


def join(own, other, after):
    return pl.pallas_call(
        join_kernel,
        in_specs=[VMEM, VMEM, HBM],
        out_specs=VMEM,
        out_shape=jax.ShapeDtypeStruct(own.shape, own.dtype),
        compiler_params=pltpu.CompilerParams(vmem_limit_bytes=4 << 20),
        name="join",
    )(in_vmem(own), in_vmem(other), in_hbm(after))


def on_device(queries, latent, out_grad, log_norms, row_dots):
    number, heads, key_width = queries.shape
    shard = latent.shape[0]
    half = number // 2

    spread = jnp.broadcast_to(latent[None], (lax.axis_size(CHIPS), shard, key_width))
    keys = lax.all_to_all(spread, CHIPS, 0, 0, tiled=True)

    def flat(queries, out_grad, stats):
        rows = number * heads
        return (
            queries.reshape(rows, key_width),
            out_grad.reshape(rows, out_grad.shape[2]),
            stats.reshape(2, rows // TILE, TILE).transpose(1, 0, 2),
        )

    mine = (queries, out_grad, jnp.stack([log_norms, row_dots]))
    theirs = flat(*[swap(array, "core") for array in mine])
    mine = flat(*mine)

    kept = lax.axis_index("y_hi").astype(jnp.int32)[None]
    sent = 1 - kept
    whole = (half, heads, key_width)
    dq_sent_theirs, dq_theirs, *sums = grads(keys, sent, theirs, halves=2, do_stays=True, before=mine)
    returned = swap(dq_sent_theirs.reshape(whole), "core")
    dq_sent_mine, *sums = grads(keys, sent, mine, sums=sums, stays=True)
    over_cores = core_sum(dq_sent_mine.reshape(whole), returned)
    received = swap(over_cores, "y_hi")
    dq_mine, dkv = grads(keys, kept, mine, sums=sums, last=True, before=[over_cores])
    returned = swap(dq_theirs.reshape(whole), "core")
    query_grad = add([dq_mine.reshape(whole), returned, received], jnp.float32, softmax_scale, resident=[False, False, True])
    parts = lax.all_to_all(dkv.reshape(-1, 2 * shard, key_width), PLANE, 0, 0, tiled=True)
    own, other = sum_parts(parts, lax.axis_index("y_lo").astype(jnp.int32)[None])
    return (query_grad, join(own, swap(other, "y_lo"), query_grad))


def solution(mesh):
    fine = Mesh(mesh.devices.reshape(4, 2, 4, 2, 2), FINE_AXES)
    query, head = ("x", "y_lo"), ("z", "core")
    in_specs = (
        P(query, head, None),
        P(FINE_AXES, None),
        P(query, head, None),
        P(query, head),
        P(query, head),
    )
    out_specs = (P(query + ("y_hi",), head, None), P(FINE_AXES, None))
    return jax.shard_map(on_device, mesh=fine, in_specs=in_specs, out_specs=out_specs, check_vma=False)
```

```python
import functools
import math

import jax
import jax.numpy as jnp
from jax import lax
from jax.experimental import pallas as pl
from jax.experimental.pallas import tpu as pltpu
from jax.sharding import Mesh, PartitionSpec as P

softmax_scale = 192.0 ** (-0.5) * (0.1 * math.log(40.0) + 1.0) ** 2
log2_e = math.log2(math.e)

FINE_AXES = ("z", "core", "x", "y_lo", "y_hi")
CHIPS = ("z", "x", "y_lo")
PLANE = ("z", "x")
TILE = 512
LANES = 128
PIECES = 4

NT = (((1,), (1,)), ((), ()))
NN = (((1,), (0,)), ((), ()))
VMEM = pl.BlockSpec(memory_space=pltpu.VMEM)
HBM = pl.BlockSpec(memory_space=pl.ANY)


def f32_dot(left, right, dims):
    return lax.dot_general(left, right, dims, preferred_element_type=jnp.float32)


def in_vmem(array):
    return pltpu.with_memory_space_constraint(array, pltpu.VMEM)


def in_hbm(array):
    return pltpu.with_memory_space_constraint(array, pltpu.HBM)


def core_sum_kernel(mine_ref, theirs_ref, out_ref):
    out_ref[...] = (mine_ref[...] + theirs_ref[...]).astype(out_ref.dtype)


def core_sum(mine, theirs):
    return pl.pallas_call(
        core_sum_kernel,
        in_specs=[VMEM, VMEM],
        out_specs=VMEM,
        out_shape=pltpu.VMEM(mine.shape, jnp.bfloat16),
        compiler_params=pltpu.CompilerParams(vmem_limit_bytes=4 << 20),
        cost_estimate=pl.CostEstimate(flops=mine.size, bytes_accessed=mine.size, transcendentals=0),
        name="core_sum",
    )(in_vmem(mine), in_vmem(theirs))


def swap(array, axis):
    return lax.ppermute(array, axis, [(0, 1), (1, 0)])


def grads_kernel(first, last, stays, do_stays, n_halves, n_before, *refs):
    refs = list(refs)
    take = lambda number: [refs.pop(0) for _ in range(number)]
    half, key_ref, q_hbm, do_hbm, stat_ref = take(5)
    sum_in = [] if first else take(2)
    take(n_before)
    dq_refs = take(n_halves)
    dkv_ref = refs.pop(0) if last else None
    key_acc, value_acc, q_tiles, sems, *refs = refs
    dkv_tiles = refs.pop() if last else None
    dq_tiles = [] if stays else [refs.pop(0)]
    do_tiles = refs
    rows, width = value_acc.shape
    key_width = key_ref.shape[-1]
    count = dq_refs[0].shape[0]
    per_half = count // TILE

    def begin(tile):
        side = half[0] if tile < per_half else 1 - half[0]
        return pl.multiple_of(side * count, TILE) + tile % per_half * TILE

    copies, results = [], []
    for tile in range(n_halves * per_half):
        at = pl.ds(begin(tile), TILE)
        pair = [pltpu.make_async_copy(q_hbm.at[at, :], q_tiles.at[tile], sems.at[0, tile])]
        if not do_stays:
            pair.append(pltpu.make_async_copy(do_hbm.at[at, :], do_tiles[0].at[tile], sems.at[1, tile]))
        for copy in pair:
            copy.start()
        copies.append(pair)

    keys = key_ref[...].reshape(rows, key_width)
    keys_t = keys.T
    for tile, pair in enumerate(copies):
        for copy in pair:
            copy.wait()
        queries = q_tiles[tile]
        douts = do_hbm[pl.ds(begin(tile), TILE), :] if do_stays else do_tiles[0][tile]
        side = half[0] if tile < per_half else 1 - half[0]
        stats = stat_ref[side * per_half + tile % per_half]
        scores = f32_dot(keys, queries, NT)
        dprobs = f32_dot(keys[:, :width], douts, NT)
        probs = jnp.exp2(scores * (softmax_scale * log2_e) - stats[0:1, :] * log2_e)
        dscores = (probs * (dprobs - stats[1:2, :])).astype(jnp.bfloat16)
        dq_at = dq_refs[tile // per_half].at[pl.ds(tile % per_half * TILE, TILE), :]
        query_part = f32_dot(keys_t, dscores, NN).T
        if stays:
            dq_at[...] = query_part
        else:
            dq_tiles[0][tile] = query_part
            result = pltpu.make_async_copy(dq_tiles[0].at[tile], dq_at, sems.at[2, tile])
            result.start()
            results.append(result)
        key_part = f32_dot(queries.T, dscores, NT)
        value_part = f32_dot(probs.astype(jnp.bfloat16), douts, NN)
        if tile > 0:
            key_acc[...] += key_part
            value_acc[...] += value_part
        elif first:
            key_acc[...] = key_part
            value_acc[...] = value_part
        else:
            key_acc[...] = sum_in[0][...] + key_part
            value_acc[...] = sum_in[1][...] + value_part
        if last and tile == len(copies) - 1:
            some = dkv_tiles.shape[0] // PIECES
            for piece in range(PIECES):
                shards = pl.ds(piece * some, some)
                at = slice(piece * rows // PIECES, (piece + 1) * rows // PIECES)
                shard = rows // dkv_tiles.shape[0]
                key_sum = key_acc[:, at].T * softmax_scale
                summed = (key_sum[:, :width] + value_acc[at, :]).astype(dkv_tiles.dtype)
                for block in range(width // LANES):
                    columns = summed[:, block * LANES : (block + 1) * LANES].reshape(some, shard, LANES)
                    dkv_tiles[shards, block * shard : (block + 1) * shard, :] = columns
                rest = key_sum[:, width:].astype(dkv_tiles.dtype).reshape(some, 2, shard // 2, LANES // 2)
                rest = jnp.concatenate([rest[:, 0], rest[:, 1]], axis=-1)
                dkv_tiles[shards, width // LANES * shard :, :] = rest
                result = pltpu.make_async_copy(dkv_tiles.at[shards], dkv_ref.at[shards], sems.at[3, piece])
                result.start()
                results.append(result)
    for result in results:
        result.wait()


def grads(keys, half, side, halves=1, sums=None, last=False, stays=False, do_stays=False, before=()):
    shards, shard, key_width = keys.shape
    rows = shards * shard
    queries, douts, stats = side
    total, width = douts.shape
    count = total // 2
    tiles = halves * count // TILE
    first = sums is None
    operands = [half, in_vmem(keys), in_hbm(queries), (in_vmem if do_stays else in_hbm)(douts), in_vmem(stats)]
    in_specs = [VMEM, HBM, VMEM if do_stays else HBM, VMEM]
    sum_shapes = [(key_width, rows), (rows, width)]
    out_shape = [(pltpu.VMEM if stays else pltpu.HBM)((count, key_width), jnp.float32)] * halves
    out_specs = [VMEM if stays else HBM] * halves
    scratch = [
        pltpu.VMEM((tiles, TILE, key_width), queries.dtype),
        pltpu.SemaphoreType.DMA((4, max(tiles, PIECES))),
    ]
    if not stays:
        scratch.append(pltpu.VMEM((tiles, TILE, key_width), jnp.float32))
    if not do_stays:
        scratch.append(pltpu.VMEM((tiles, TILE, width), douts.dtype))
    aliases = {}
    if not first:
        if not last:
            aliases = {len(operands): halves, len(operands) + 1: halves + 1}
        operands += [in_vmem(array) for array in sums]
        in_specs += [VMEM, VMEM]
    if last:
        packed = (shards, shard * key_width // LANES, LANES)
        out_shape.append(pltpu.HBM(packed, keys.dtype))
        out_specs.append(HBM)
        scratch = [pltpu.VMEM(shape, jnp.float32) for shape in sum_shapes] + scratch
        scratch.append(pltpu.VMEM(packed, keys.dtype))
    else:
        out_shape += [pltpu.VMEM(shape, jnp.float32) for shape in sum_shapes]
        out_specs += [VMEM, VMEM]
    place, spec = (in_hbm, HBM) if first else (in_vmem, VMEM)
    operands += [place(array) for array in before]
    in_specs += [spec] * len(before)
    return pl.pallas_call(
        functools.partial(grads_kernel, first, last, stays, do_stays, halves, len(before)),
        grid_spec=pltpu.PrefetchScalarGridSpec(
            num_scalar_prefetch=1, grid=(1,), in_specs=in_specs, out_specs=out_specs, scratch_shapes=scratch
        ),
        out_shape=out_shape,
        input_output_aliases=aliases,
        compiler_params=pltpu.CompilerParams(vmem_limit_bytes=32 << 20),
        cost_estimate=pl.CostEstimate(flops=rows * count, bytes_accessed=rows * key_width * 2, transcendentals=rows),
        name="grads",
    )(*operands)


def add_kernel(out_scale, *refs):
    *addends, out_ref = refs
    rows = out_ref.shape[0]
    at = pl.ds(pl.program_id(0) * rows, rows)
    parts = [addend[...] if addend.shape[0] == rows else addend[at] for addend in addends]
    total = parts[0].astype(jnp.float32)
    for part in parts[1:]:
        total += part.astype(jnp.float32)
    out_ref[...] = (total * out_scale if out_scale else total).astype(out_ref.dtype)


def add(addends, dtype, out_scale=None, resident=None):
    rows, heads, key_width = addends[0].shape
    steps = 4
    resident = resident or [True] * len(addends)
    block = pl.BlockSpec((rows // steps, heads, key_width), lambda i: (i, 0, 0))
    return pl.pallas_call(
        functools.partial(add_kernel, out_scale),
        grid=(steps,),
        in_specs=[VMEM if stays else block for stays in resident],
        out_specs=block,
        out_shape=pltpu.HBM((rows, heads, key_width), dtype),
        compiler_params=pltpu.CompilerParams(vmem_limit_bytes=12 << 20),
        cost_estimate=pl.CostEstimate(
            flops=rows * heads * key_width * 2, bytes_accessed=rows * heads * key_width * 4, transcendentals=0
        ),
        name="add",
    )(*[(in_vmem if stays else in_hbm)(addend) for addend, stays in zip(addends, resident)])


def sum_kernel(place, parts_ref, mine_ref, other_ref):
    shard, key_width = mine_ref.shape
    packed = parts_ref.shape[1] // 2
    blocks = key_width // LANES
    for out_ref, at in ((mine_ref, place[0]), (other_ref, 1 - place[0])):
        rows = pl.ds(pl.multiple_of(at * packed, shard // 2), packed)
        total = parts_ref[0, rows, :].astype(jnp.float32)
        for part in range(1, parts_ref.shape[0]):
            total += parts_ref[part, rows, :].astype(jnp.float32)
        for block in range(blocks):
            out_ref[:, block * LANES : (block + 1) * LANES] = total[block * shard : (block + 1) * shard, :]
        rest = total[blocks * shard :, :]
        out_ref[: shard // 2, blocks * LANES :] = rest[:, : LANES // 2]
        out_ref[shard // 2 :, blocks * LANES :] = rest[:, LANES // 2 :]


def sum_parts(parts, place, shape):
    return pl.pallas_call(
        sum_kernel,
        grid_spec=pltpu.PrefetchScalarGridSpec(num_scalar_prefetch=1, grid=(1,), in_specs=[VMEM], out_specs=[VMEM, VMEM]),
        out_shape=[pltpu.VMEM(shape, jnp.float32)] * 2,
        compiler_params=pltpu.CompilerParams(vmem_limit_bytes=4 << 20),
        name="sum_parts",
    )(place, in_vmem(parts))


def join_kernel(own_ref, other_ref, after_ref, out_ref):
    out_ref[...] = own_ref[...] + other_ref[...]


def join(own, other, after):
    return pl.pallas_call(
        join_kernel,
        in_specs=[VMEM, VMEM, HBM],
        out_specs=VMEM,
        out_shape=jax.ShapeDtypeStruct(own.shape, own.dtype),
        compiler_params=pltpu.CompilerParams(vmem_limit_bytes=4 << 20),
        name="join",
    )(in_vmem(own), in_vmem(other), in_hbm(after))


def on_device(queries, latent, out_grad, log_norms, row_dots):
    number, heads, key_width = queries.shape
    shard = latent.shape[0]
    half = number // 2

    spread = jnp.broadcast_to(latent[None], (lax.axis_size(CHIPS), shard, key_width))
    keys = lax.all_to_all(spread, CHIPS, 0, 0, tiled=True)

    def flat(queries, out_grad, stats):
        rows = number * heads
        return (
            queries.reshape(rows, key_width),
            out_grad.reshape(rows, out_grad.shape[2]),
            stats.reshape(2, rows // TILE, TILE).transpose(1, 0, 2),
        )

    mine = (queries, out_grad, jnp.stack([log_norms, row_dots]))
    theirs = flat(*[swap(array, "core") for array in mine])
    mine = flat(*mine)

    kept = lax.axis_index("y_hi").astype(jnp.int32)[None]
    sent = 1 - kept
    whole = (half, heads, key_width)
    dq_sent_theirs, dq_theirs, *sums = grads(keys, sent, theirs, halves=2, do_stays=True, before=mine)
    returned = swap(dq_sent_theirs.reshape(whole), "core")
    dq_sent_mine, *sums = grads(keys, sent, mine, sums=sums, stays=True)
    over_cores = core_sum(dq_sent_mine.reshape(whole), returned)
    received = swap(over_cores, "y_hi")
    dq_mine, dkv = grads(keys, kept, mine, sums=sums, last=True, before=[over_cores])
    returned = swap(dq_theirs.reshape(whole), "core")
    query_grad = add([dq_mine.reshape(whole), returned, received], jnp.float32, softmax_scale, resident=[False, False, True])
    parts = lax.all_to_all(dkv.reshape(-1, 2 * dkv.shape[1], LANES), PLANE, 0, 0, tiled=True)
    own, other = sum_parts(parts, lax.axis_index("y_lo").astype(jnp.int32)[None], latent.shape)
    return (query_grad, join(own, swap(other, "y_lo"), query_grad))


def solution(mesh):
    fine = Mesh(mesh.devices.reshape(4, 2, 4, 2, 2), FINE_AXES)
    query, head = ("x", "y_lo"), ("z", "core")
    in_specs = (
        P(query, head, None),
        P(FINE_AXES, None),
        P(query, head, None),
        P(query, head),
        P(query, head),
    )
    out_specs = (P(query + ("y_hi",), head, None), P(FINE_AXES, None))
    return jax.shard_map(on_device, mesh=fine, in_specs=in_specs, out_specs=out_specs, check_vma=False)
```

```python
import functools
import math

import jax
import jax.numpy as jnp
from jax import lax
from jax.experimental import pallas as pl
from jax.experimental.pallas import tpu as pltpu
from jax.sharding import Mesh, PartitionSpec as P

softmax_scale = 192.0 ** (-0.5) * (0.1 * math.log(40.0) + 1.0) ** 2
log2_e = math.log2(math.e)

FINE_AXES = ("z", "core", "x", "y_lo", "y_hi")
CHIPS = ("z", "x", "y_lo")
PLANE = ("z", "x")
TILE = 512
LANES = 128
PIECES = 4

NT = (((1,), (1,)), ((), ()))
NN = (((1,), (0,)), ((), ()))
VMEM = pl.BlockSpec(memory_space=pltpu.VMEM)
HBM = pl.BlockSpec(memory_space=pl.ANY)


def f32_dot(left, right, dims):
    return lax.dot_general(left, right, dims, preferred_element_type=jnp.float32)


def in_vmem(array):
    return pltpu.with_memory_space_constraint(array, pltpu.VMEM)


def in_hbm(array):
    return pltpu.with_memory_space_constraint(array, pltpu.HBM)


def core_sum_kernel(mine_ref, theirs_ref, out_ref):
    out_ref[...] = (mine_ref[...] + theirs_ref[...]).astype(out_ref.dtype)


def core_sum(mine, theirs):
    return pl.pallas_call(
        core_sum_kernel,
        in_specs=[VMEM, VMEM],
        out_specs=VMEM,
        out_shape=pltpu.VMEM(mine.shape, jnp.bfloat16),
        compiler_params=pltpu.CompilerParams(vmem_limit_bytes=4 << 20),
        cost_estimate=pl.CostEstimate(flops=mine.size, bytes_accessed=mine.size, transcendentals=0),
        name="core_sum",
    )(in_vmem(mine), in_vmem(theirs))


def swap(array, axis):
    return lax.ppermute(array, axis, [(0, 1), (1, 0)])


def pack_kernel(latent_ref, packed_ref):
    shard, key_width = latent_ref.shape
    blocks = key_width // LANES
    for block in range(blocks):
        packed_ref[block * shard : (block + 1) * shard, :] = latent_ref[:, block * LANES : (block + 1) * LANES]
    rest = latent_ref[:, blocks * LANES :]
    packed_ref[blocks * shard :, :] = jnp.concatenate([rest[: shard // 2], rest[shard // 2 :]], axis=-1)


def pack(latent):
    return pl.pallas_call(
        pack_kernel,
        in_specs=[VMEM],
        out_specs=VMEM,
        out_shape=jax.ShapeDtypeStruct((latent.size // LANES, LANES), latent.dtype),
        compiler_params=pltpu.CompilerParams(vmem_limit_bytes=4 << 20),
        name="pack",
    )(latent)


def grads_kernel(first, last, stays, do_stays, n_halves, n_before, *refs):
    refs = list(refs)
    take = lambda number: [refs.pop(0) for _ in range(number)]
    half, key_ref, q_hbm, do_hbm, stat_ref = take(5)
    sum_in = [] if first else take(2)
    take(n_before)
    dq_refs = take(n_halves)
    dkv_ref = refs.pop(0) if last else None
    keys_ref = refs.pop(0) if first else key_ref
    key_acc, value_acc, q_tiles, sems, *refs = refs
    dkv_tiles = refs.pop() if last else None
    dq_tiles = [] if stays else [refs.pop(0)]
    do_tiles = refs
    rows, width = value_acc.shape
    key_width = keys_ref.shape[-1]
    count = dq_refs[0].shape[0]
    per_half = count // TILE

    def begin(tile):
        side = half[0] if tile < per_half else 1 - half[0]
        return pl.multiple_of(side * count, TILE) + tile % per_half * TILE

    copies, results = [], []
    for tile in range(n_halves * per_half):
        at = pl.ds(begin(tile), TILE)
        pair = [pltpu.make_async_copy(q_hbm.at[at, :], q_tiles.at[tile], sems.at[0, tile])]
        if not do_stays:
            pair.append(pltpu.make_async_copy(do_hbm.at[at, :], do_tiles[0].at[tile], sems.at[1, tile]))
        for copy in pair:
            copy.start()
        copies.append(pair)

    if first:
        blocks = width // LANES
        shards = key_ref.shape[0]
        shard = rows // shards
        for block in range(blocks):
            columns = key_ref[:, block * shard : (block + 1) * shard, :].reshape(rows, LANES)
            keys_ref[:, block * LANES : (block + 1) * LANES] = columns
        rest = key_ref[:, blocks * shard :, :]
        rest = jnp.stack([rest[:, :, : LANES // 2], rest[:, :, LANES // 2 :]], axis=1)
        keys_ref[:, width:] = rest.reshape(rows, key_width - width)
    keys = keys_ref[...]
    keys_t = keys.T
    for tile, pair in enumerate(copies):
        for copy in pair:
            copy.wait()
        queries = q_tiles[tile]
        douts = do_hbm[pl.ds(begin(tile), TILE), :] if do_stays else do_tiles[0][tile]
        side = half[0] if tile < per_half else 1 - half[0]
        stats = stat_ref[side * per_half + tile % per_half]
        scores = f32_dot(keys, queries, NT)
        dprobs = f32_dot(keys[:, :width], douts, NT)
        probs = jnp.exp2(scores * (softmax_scale * log2_e) - stats[0:1, :] * log2_e)
        dscores = (probs * (dprobs - stats[1:2, :])).astype(jnp.bfloat16)
        dq_at = dq_refs[tile // per_half].at[pl.ds(tile % per_half * TILE, TILE), :]
        query_part = f32_dot(keys_t, dscores, NN).T
        if stays:
            dq_at[...] = query_part
        else:
            dq_tiles[0][tile] = query_part
            result = pltpu.make_async_copy(dq_tiles[0].at[tile], dq_at, sems.at[2, tile])
            result.start()
            results.append(result)
        key_part = f32_dot(queries.T, dscores, NT)
        value_part = f32_dot(probs.astype(jnp.bfloat16), douts, NN)
        if tile > 0:
            key_acc[...] += key_part
            value_acc[...] += value_part
        elif first:
            key_acc[...] = key_part
            value_acc[...] = value_part
        else:
            key_acc[...] = sum_in[0][...] + key_part
            value_acc[...] = sum_in[1][...] + value_part
        if last and tile == len(copies) - 1:
            some = dkv_tiles.shape[0] // PIECES
            for piece in range(PIECES):
                shards = pl.ds(piece * some, some)
                at = slice(piece * rows // PIECES, (piece + 1) * rows // PIECES)
                shard = rows // dkv_tiles.shape[0]
                key_sum = key_acc[:, at].T * softmax_scale
                summed = (key_sum[:, :width] + value_acc[at, :]).astype(dkv_tiles.dtype)
                for block in range(width // LANES):
                    columns = summed[:, block * LANES : (block + 1) * LANES].reshape(some, shard, LANES)
                    dkv_tiles[shards, block * shard : (block + 1) * shard, :] = columns
                rest = key_sum[:, width:].astype(dkv_tiles.dtype).reshape(some, 2, shard // 2, LANES // 2)
                rest = jnp.concatenate([rest[:, 0], rest[:, 1]], axis=-1)
                dkv_tiles[shards, width // LANES * shard :, :] = rest
                result = pltpu.make_async_copy(dkv_tiles.at[shards], dkv_ref.at[shards], sems.at[3, piece])
                result.start()
                results.append(result)
    for result in results:
        result.wait()


def grads(keys, half, side, halves=1, sums=None, shards=0, stays=False, do_stays=False, before=()):
    queries, douts, stats = side
    key_width = queries.shape[1]
    rows = keys.size // key_width
    total, width = douts.shape
    count = total // 2
    tiles = halves * count // TILE
    first, last = sums is None, shards > 0
    operands = [half, in_vmem(keys), in_hbm(queries), (in_vmem if do_stays else in_hbm)(douts), in_vmem(stats)]
    in_specs = [VMEM, HBM, VMEM if do_stays else HBM, VMEM]
    sum_shapes = [(key_width, rows), (rows, width)]
    out_shape = [(pltpu.VMEM if stays else pltpu.HBM)((count, key_width), jnp.float32)] * halves
    out_specs = [VMEM if stays else HBM] * halves
    scratch = [
        pltpu.VMEM((tiles, TILE, key_width), queries.dtype),
        pltpu.SemaphoreType.DMA((4, max(tiles, PIECES))),
    ]
    if not stays:
        scratch.append(pltpu.VMEM((tiles, TILE, key_width), jnp.float32))
    if not do_stays:
        scratch.append(pltpu.VMEM((tiles, TILE, width), douts.dtype))
    aliases = {}
    if not first:
        if not last:
            aliases = {len(operands): halves, len(operands) + 1: halves + 1}
        operands += [in_vmem(array) for array in sums]
        in_specs += [VMEM, VMEM]
    if last:
        packed = (shards, rows // shards * key_width // LANES, LANES)
        out_shape.append(pltpu.HBM(packed, keys.dtype))
        out_specs.append(HBM)
        scratch = [pltpu.VMEM(shape, jnp.float32) for shape in sum_shapes] + scratch
        scratch.append(pltpu.VMEM(packed, keys.dtype))
    else:
        if first:
            out_shape.append(pltpu.VMEM((rows, key_width), keys.dtype))
            out_specs.append(VMEM)
        out_shape += [pltpu.VMEM(shape, jnp.float32) for shape in sum_shapes]
        out_specs += [VMEM, VMEM]
    place, spec = (in_hbm, HBM) if first else (in_vmem, VMEM)
    operands += [place(array) for array in before]
    in_specs += [spec] * len(before)
    return pl.pallas_call(
        functools.partial(grads_kernel, first, last, stays, do_stays, halves, len(before)),
        grid_spec=pltpu.PrefetchScalarGridSpec(
            num_scalar_prefetch=1, grid=(1,), in_specs=in_specs, out_specs=out_specs, scratch_shapes=scratch
        ),
        out_shape=out_shape,
        input_output_aliases=aliases,
        compiler_params=pltpu.CompilerParams(vmem_limit_bytes=32 << 20),
        cost_estimate=pl.CostEstimate(flops=rows * count, bytes_accessed=rows * key_width * 2, transcendentals=rows),
        name="grads",
    )(*operands)


def add_kernel(out_scale, *refs):
    *addends, out_ref = refs
    rows = out_ref.shape[0]
    at = pl.ds(pl.program_id(0) * rows, rows)
    parts = [addend[...] if addend.shape[0] == rows else addend[at] for addend in addends]
    total = parts[0].astype(jnp.float32)
    for part in parts[1:]:
        total += part.astype(jnp.float32)
    out_ref[...] = (total * out_scale if out_scale else total).astype(out_ref.dtype)


def add(addends, dtype, out_scale=None, resident=None):
    rows, heads, key_width = addends[0].shape
    steps = 4
    resident = resident or [True] * len(addends)
    block = pl.BlockSpec((rows // steps, heads, key_width), lambda i: (i, 0, 0))
    return pl.pallas_call(
        functools.partial(add_kernel, out_scale),
        grid=(steps,),
        in_specs=[VMEM if stays else block for stays in resident],
        out_specs=block,
        out_shape=pltpu.HBM((rows, heads, key_width), dtype),
        compiler_params=pltpu.CompilerParams(vmem_limit_bytes=12 << 20),
        cost_estimate=pl.CostEstimate(
            flops=rows * heads * key_width * 2, bytes_accessed=rows * heads * key_width * 4, transcendentals=0
        ),
        name="add",
    )(*[(in_vmem if stays else in_hbm)(addend) for addend, stays in zip(addends, resident)])


def sum_kernel(place, parts_ref, mine_ref, other_ref):
    shard, key_width = mine_ref.shape
    packed = parts_ref.shape[1] // 2
    blocks = key_width // LANES
    for out_ref, at in ((mine_ref, place[0]), (other_ref, 1 - place[0])):
        rows = pl.ds(pl.multiple_of(at * packed, shard // 2), packed)
        total = parts_ref[0, rows, :].astype(jnp.float32)
        for part in range(1, parts_ref.shape[0]):
            total += parts_ref[part, rows, :].astype(jnp.float32)
        for block in range(blocks):
            out_ref[:, block * LANES : (block + 1) * LANES] = total[block * shard : (block + 1) * shard, :]
        rest = total[blocks * shard :, :]
        out_ref[: shard // 2, blocks * LANES :] = rest[:, : LANES // 2]
        out_ref[shard // 2 :, blocks * LANES :] = rest[:, LANES // 2 :]


def sum_parts(parts, place, shape):
    return pl.pallas_call(
        sum_kernel,
        grid_spec=pltpu.PrefetchScalarGridSpec(num_scalar_prefetch=1, grid=(1,), in_specs=[VMEM], out_specs=[VMEM, VMEM]),
        out_shape=[pltpu.VMEM(shape, jnp.float32)] * 2,
        compiler_params=pltpu.CompilerParams(vmem_limit_bytes=4 << 20),
        name="sum_parts",
    )(place, in_vmem(parts))


def join_kernel(own_ref, other_ref, after_ref, out_ref):
    out_ref[...] = own_ref[...] + other_ref[...]


def join(own, other, after):
    return pl.pallas_call(
        join_kernel,
        in_specs=[VMEM, VMEM, HBM],
        out_specs=VMEM,
        out_shape=jax.ShapeDtypeStruct(own.shape, own.dtype),
        compiler_params=pltpu.CompilerParams(vmem_limit_bytes=4 << 20),
        name="join",
    )(in_vmem(own), in_vmem(other), in_hbm(after))


def on_device(queries, latent, out_grad, log_norms, row_dots):
    number, heads, key_width = queries.shape
    half = number // 2

    chips = lax.axis_size(CHIPS)
    packed = pack(latent)
    keys = lax.all_to_all(jnp.broadcast_to(packed[None], (chips, *packed.shape)), CHIPS, 0, 0, tiled=True)

    def flat(queries, out_grad, stats):
        rows = number * heads
        return (
            queries.reshape(rows, key_width),
            out_grad.reshape(rows, out_grad.shape[2]),
            stats.reshape(2, rows // TILE, TILE).transpose(1, 0, 2),
        )

    mine = (queries, out_grad, jnp.stack([log_norms, row_dots]))
    theirs = flat(*[swap(array, "core") for array in mine])
    mine = flat(*mine)

    kept = lax.axis_index("y_hi").astype(jnp.int32)[None]
    sent = 1 - kept
    whole = (half, heads, key_width)
    dq_sent_theirs, dq_theirs, keys, *sums = grads(keys, sent, theirs, halves=2, do_stays=True, before=mine)
    returned = swap(dq_sent_theirs.reshape(whole), "core")
    dq_sent_mine, *sums = grads(keys, sent, mine, sums=sums, stays=True)
    over_cores = core_sum(dq_sent_mine.reshape(whole), returned)
    received = swap(over_cores, "y_hi")
    dq_mine, dkv = grads(keys, kept, mine, sums=sums, shards=chips, before=[over_cores])
    returned = swap(dq_theirs.reshape(whole), "core")
    query_grad = add([dq_mine.reshape(whole), returned, received], jnp.float32, softmax_scale, resident=[False, False, True])
    parts = lax.all_to_all(dkv.reshape(-1, 2 * dkv.shape[1], LANES), PLANE, 0, 0, tiled=True)
    own, other = sum_parts(parts, lax.axis_index("y_lo").astype(jnp.int32)[None], latent.shape)
    return (query_grad, join(own, swap(other, "y_lo"), query_grad))


def solution(mesh):
    fine = Mesh(mesh.devices.reshape(4, 2, 4, 2, 2), FINE_AXES)
    query, head = ("x", "y_lo"), ("z", "core")
    in_specs = (
        P(query, head, None),
        P(FINE_AXES, None),
        P(query, head, None),
        P(query, head),
        P(query, head),
    )
    out_specs = (P(query + ("y_hi",), head, None), P(FINE_AXES, None))
    return jax.shard_map(on_device, mesh=fine, in_specs=in_specs, out_specs=out_specs, check_vma=False)
```

```python
import functools
import math

import jax
import jax.numpy as jnp
from jax import lax
from jax.experimental import pallas as pl
from jax.experimental.pallas import tpu as pltpu
from jax.sharding import Mesh, PartitionSpec as P

softmax_scale = 192.0 ** (-0.5) * (0.1 * math.log(40.0) + 1.0) ** 2
log2_e = math.log2(math.e)

FINE_AXES = ("z", "core", "x", "y_lo", "y_hi")
CHIPS = ("z", "x", "y_lo")
PLANE = ("z", "x")
TILE = 512
LANES = 128
PIECES = 4

NT = (((1,), (1,)), ((), ()))
NN = (((1,), (0,)), ((), ()))
VMEM = pl.BlockSpec(memory_space=pltpu.VMEM)
HBM = pl.BlockSpec(memory_space=pl.ANY)


def f32_dot(left, right, dims):
    return lax.dot_general(left, right, dims, preferred_element_type=jnp.float32)


def in_vmem(array):
    return pltpu.with_memory_space_constraint(array, pltpu.VMEM)


def in_hbm(array):
    return pltpu.with_memory_space_constraint(array, pltpu.HBM)


def core_sum_kernel(mine_ref, theirs_ref, out_ref):
    out_ref[...] = (mine_ref[...] + theirs_ref[...]).astype(out_ref.dtype)


def core_sum(mine, theirs):
    return pl.pallas_call(
        core_sum_kernel,
        in_specs=[VMEM, VMEM],
        out_specs=VMEM,
        out_shape=pltpu.VMEM(mine.shape, jnp.bfloat16),
        compiler_params=pltpu.CompilerParams(vmem_limit_bytes=4 << 20),
        cost_estimate=pl.CostEstimate(flops=mine.size, bytes_accessed=mine.size, transcendentals=0),
        name="core_sum",
    )(in_vmem(mine), in_vmem(theirs))


def swap(array, axis):
    return lax.ppermute(array, axis, [(0, 1), (1, 0)])


def pack_kernel(latent_ref, packed_ref):
    shard, key_width = latent_ref.shape
    blocks = key_width // LANES
    for block in range(blocks):
        packed_ref[block * shard : (block + 1) * shard, :] = latent_ref[:, block * LANES : (block + 1) * LANES]
    rest = latent_ref[:, blocks * LANES :]
    packed_ref[blocks * shard :, :] = jnp.concatenate([rest[: shard // 2], rest[shard // 2 :]], axis=-1)


def pack(latent):
    return pl.pallas_call(
        pack_kernel,
        in_specs=[VMEM],
        out_specs=VMEM,
        out_shape=jax.ShapeDtypeStruct((latent.size // LANES, LANES), latent.dtype),
        compiler_params=pltpu.CompilerParams(vmem_limit_bytes=4 << 20),
        name="pack",
    )(latent)


def grads_kernel(first, last, stays, do_stays, n_halves, n_before, *refs):
    refs = list(refs)
    take = lambda number: [refs.pop(0) for _ in range(number)]
    half, key_ref, q_hbm, do_hbm, stat_ref = take(5)
    sum_in = [] if first else take(2)
    take(n_before)
    dq_refs = take(n_halves)
    dkv_ref = refs.pop(0) if last else None
    keys_ref = refs.pop(0) if first else key_ref
    key_acc, value_acc, q_tiles, sems, *refs = refs
    dkv_tiles = refs.pop() if last else None
    dq_tiles = [] if stays else [refs.pop(0)]
    do_tiles = refs
    rows, width = value_acc.shape
    key_width = keys_ref.shape[-1]
    count = dq_refs[0].shape[0]
    per_half = count // TILE

    def begin(tile):
        side = half[0] if tile < per_half else 1 - half[0]
        return pl.multiple_of(side * count, TILE) + tile % per_half * TILE

    copies, results = [], []
    for tile in range(n_halves * per_half):
        at = pl.ds(begin(tile), TILE)
        pair = [pltpu.make_async_copy(q_hbm.at[at, :], q_tiles.at[tile], sems.at[0, tile])]
        if not do_stays:
            pair.append(pltpu.make_async_copy(do_hbm.at[at, :], do_tiles[0].at[tile], sems.at[1, tile]))
        for copy in pair:
            copy.start()
        copies.append(pair)

    if first:
        blocks = width // LANES
        shards = key_ref.shape[0]
        shard = rows // shards
        for block in range(blocks):
            columns = key_ref[:, block * shard : (block + 1) * shard, :].reshape(rows, LANES)
            keys_ref[:, block * LANES : (block + 1) * LANES] = columns
        rest = key_ref[:, blocks * shard :, :]
        rest = jnp.stack([rest[:, :, : LANES // 2], rest[:, :, LANES // 2 :]], axis=1)
        keys_ref[:, width:] = rest.reshape(rows, key_width - width)
    keys = keys_ref[...]
    keys_t = keys.T
    for tile, pair in enumerate(copies):
        for copy in pair:
            copy.wait()
        queries = q_tiles[tile]
        douts = do_hbm[pl.ds(begin(tile), TILE), :] if do_stays else do_tiles[0][tile]
        side = half[0] if tile < per_half else 1 - half[0]
        stats = stat_ref[side * per_half + tile % per_half]
        scores = f32_dot(keys, queries, NT)
        dprobs = f32_dot(keys[:, :width], douts, NT)
        probs = jnp.exp2(scores * (softmax_scale * log2_e) - stats[0:1, :] * log2_e)
        dscores = (probs * (dprobs - stats[1:2, :])).astype(jnp.bfloat16)
        dq_at = dq_refs[tile // per_half].at[pl.ds(tile % per_half * TILE, TILE), :]
        query_part = f32_dot(keys_t, dscores, NN).T
        if stays:
            dq_at[...] = query_part
        else:
            dq_tiles[0][tile] = query_part
            result = pltpu.make_async_copy(dq_tiles[0].at[tile], dq_at, sems.at[2, tile])
            result.start()
            results.append(result)
        key_part = f32_dot(queries.T, dscores, NT)
        value_part = f32_dot(probs.astype(jnp.bfloat16), douts, NN)
        if tile > 0:
            key_acc[...] += key_part
            value_acc[...] += value_part
        elif first:
            key_acc[...] = key_part
            value_acc[...] = value_part
        else:
            key_acc[...] = sum_in[0][...] + key_part
            value_acc[...] = sum_in[1][...] + value_part
        if last and tile == len(copies) - 1:
            some = dkv_tiles.shape[0] // PIECES
            for piece in range(PIECES):
                shards = pl.ds(piece * some, some)
                at = slice(piece * rows // PIECES, (piece + 1) * rows // PIECES)
                shard = rows // dkv_tiles.shape[0]
                key_sum = key_acc[:, at].T * softmax_scale
                summed = (key_sum[:, :width] + value_acc[at, :]).astype(dkv_tiles.dtype)
                for block in range(width // LANES):
                    columns = summed[:, block * LANES : (block + 1) * LANES].reshape(some, shard, LANES)
                    dkv_tiles[shards, block * shard : (block + 1) * shard, :] = columns
                rest = key_sum[:, width:].astype(dkv_tiles.dtype).reshape(some, 2, shard // 2, LANES // 2)
                rest = jnp.concatenate([rest[:, 0], rest[:, 1]], axis=-1)
                dkv_tiles[shards, width // LANES * shard :, :] = rest
                result = pltpu.make_async_copy(dkv_tiles.at[shards], dkv_ref.at[shards], sems.at[3, piece])
                result.start()
                results.append(result)
    for result in results:
        result.wait()


def grads(keys, half, side, halves=1, sums=None, shards=0, stays=False, do_stays=False, before=()):
    queries, douts, stats = side
    key_width = queries.shape[1]
    rows = keys.size // key_width
    total, width = douts.shape
    count = total // 2
    tiles = halves * count // TILE
    first, last = sums is None, shards > 0
    operands = [half, in_vmem(keys), in_hbm(queries), (in_vmem if do_stays else in_hbm)(douts), in_vmem(stats)]
    in_specs = [VMEM, HBM, VMEM if do_stays else HBM, VMEM]
    sum_shapes = [(key_width, rows), (rows, width)]
    out_shape = [(pltpu.VMEM if stays else pltpu.HBM)((count, key_width), jnp.float32)] * halves
    out_specs = [VMEM if stays else HBM] * halves
    scratch = [
        pltpu.VMEM((tiles, TILE, key_width), queries.dtype),
        pltpu.SemaphoreType.DMA((4, max(tiles, PIECES))),
    ]
    if not stays:
        scratch.append(pltpu.VMEM((tiles, TILE, key_width), jnp.float32))
    if not do_stays:
        scratch.append(pltpu.VMEM((tiles, TILE, width), douts.dtype))
    aliases = {}
    if not first:
        if not last:
            aliases = {len(operands): halves, len(operands) + 1: halves + 1}
        operands += [in_vmem(array) for array in sums]
        in_specs += [VMEM, VMEM]
    if last:
        packed = (shards, rows // shards * key_width // LANES, LANES)
        out_shape.append(pltpu.HBM(packed, keys.dtype))
        out_specs.append(HBM)
        scratch = [pltpu.VMEM(shape, jnp.float32) for shape in sum_shapes] + scratch
        scratch.append(pltpu.VMEM(packed, keys.dtype))
    else:
        if first:
            out_shape.append(pltpu.VMEM((rows, key_width), keys.dtype))
            out_specs.append(VMEM)
        out_shape += [pltpu.VMEM(shape, jnp.float32) for shape in sum_shapes]
        out_specs += [VMEM, VMEM]
    place, spec = (in_hbm, HBM) if first else (in_vmem, VMEM)
    operands += [place(array) for array in before]
    in_specs += [spec] * len(before)
    return pl.pallas_call(
        functools.partial(grads_kernel, first, last, stays, do_stays, halves, len(before)),
        grid_spec=pltpu.PrefetchScalarGridSpec(
            num_scalar_prefetch=1, grid=(1,), in_specs=in_specs, out_specs=out_specs, scratch_shapes=scratch
        ),
        out_shape=out_shape,
        input_output_aliases=aliases,
        compiler_params=pltpu.CompilerParams(vmem_limit_bytes=32 << 20),
        cost_estimate=pl.CostEstimate(flops=rows * count, bytes_accessed=rows * key_width * 2, transcendentals=rows),
        name="grads",
    )(*operands)


def add_kernel(out_scale, *refs):
    *addends, out_ref = refs
    rows = out_ref.shape[0]
    at = pl.ds(pl.program_id(0) * rows, rows)
    parts = [addend[...] if addend.shape[0] == rows else addend[at] for addend in addends]
    total = parts[0].astype(jnp.float32)
    for part in parts[1:]:
        total += part.astype(jnp.float32)
    out_ref[...] = (total * out_scale if out_scale else total).astype(out_ref.dtype)


def add(addends, dtype, out_scale=None, resident=None):
    rows, heads, key_width = addends[0].shape
    steps = 2
    resident = resident or [True] * len(addends)
    block = pl.BlockSpec((rows // steps, heads, key_width), lambda i: (i, 0, 0))
    return pl.pallas_call(
        functools.partial(add_kernel, out_scale),
        grid=(steps,),
        in_specs=[VMEM if stays else block for stays in resident],
        out_specs=block,
        out_shape=pltpu.HBM((rows, heads, key_width), dtype),
        compiler_params=pltpu.CompilerParams(vmem_limit_bytes=12 << 20),
        cost_estimate=pl.CostEstimate(
            flops=rows * heads * key_width * 2, bytes_accessed=rows * heads * key_width * 4, transcendentals=0
        ),
        name="add",
    )(*[(in_vmem if stays else in_hbm)(addend) for addend, stays in zip(addends, resident)])


def sum_kernel(place, parts_ref, mine_ref, other_ref):
    shard, key_width = mine_ref.shape
    packed = parts_ref.shape[1] // 2
    blocks = key_width // LANES
    for out_ref, at in ((mine_ref, place[0]), (other_ref, 1 - place[0])):
        rows = pl.ds(pl.multiple_of(at * packed, shard // 2), packed)
        total = parts_ref[0, rows, :].astype(jnp.float32)
        for part in range(1, parts_ref.shape[0]):
            total += parts_ref[part, rows, :].astype(jnp.float32)
        for block in range(blocks):
            out_ref[:, block * LANES : (block + 1) * LANES] = total[block * shard : (block + 1) * shard, :]
        rest = total[blocks * shard :, :]
        out_ref[: shard // 2, blocks * LANES :] = rest[:, : LANES // 2]
        out_ref[shard // 2 :, blocks * LANES :] = rest[:, LANES // 2 :]


def sum_parts(parts, place, shape):
    return pl.pallas_call(
        sum_kernel,
        grid_spec=pltpu.PrefetchScalarGridSpec(num_scalar_prefetch=1, grid=(1,), in_specs=[VMEM], out_specs=[VMEM, VMEM]),
        out_shape=[pltpu.VMEM(shape, jnp.float32)] * 2,
        compiler_params=pltpu.CompilerParams(vmem_limit_bytes=4 << 20),
        name="sum_parts",
    )(place, in_vmem(parts))


def join_kernel(own_ref, other_ref, after_ref, out_ref):
    out_ref[...] = own_ref[...] + other_ref[...]


def join(own, other, after):
    return pl.pallas_call(
        join_kernel,
        in_specs=[VMEM, VMEM, HBM],
        out_specs=VMEM,
        out_shape=jax.ShapeDtypeStruct(own.shape, own.dtype),
        compiler_params=pltpu.CompilerParams(vmem_limit_bytes=4 << 20),
        name="join",
    )(in_vmem(own), in_vmem(other), in_hbm(after))


def on_device(queries, latent, out_grad, log_norms, row_dots):
    number, heads, key_width = queries.shape
    half = number // 2

    chips = lax.axis_size(CHIPS)
    packed = pack(latent)
    keys = lax.all_to_all(jnp.broadcast_to(packed[None], (chips, *packed.shape)), CHIPS, 0, 0, tiled=True)

    def flat(queries, out_grad, stats):
        rows = number * heads
        return (
            queries.reshape(rows, key_width),
            out_grad.reshape(rows, out_grad.shape[2]),
            stats.reshape(2, rows // TILE, TILE).transpose(1, 0, 2),
        )

    mine = (queries, out_grad, jnp.stack([log_norms, row_dots]))
    theirs = flat(*[swap(array, "core") for array in mine])
    mine = flat(*mine)

    kept = lax.axis_index("y_hi").astype(jnp.int32)[None]
    sent = 1 - kept
    whole = (half, heads, key_width)
    dq_sent_theirs, dq_theirs, keys, *sums = grads(keys, sent, theirs, halves=2, do_stays=True, before=mine)
    returned = swap(dq_sent_theirs.reshape(whole), "core")
    dq_sent_mine, *sums = grads(keys, sent, mine, sums=sums, stays=True)
    over_cores = core_sum(dq_sent_mine.reshape(whole), returned)
    received = swap(over_cores, "y_hi")
    dq_mine, dkv = grads(keys, kept, mine, sums=sums, shards=chips, before=[over_cores])
    returned = swap(dq_theirs.reshape(whole), "core")
    query_grad = add([dq_mine.reshape(whole), returned, received], jnp.float32, softmax_scale, resident=[False, False, True])
    parts = lax.all_to_all(dkv.reshape(-1, 2 * dkv.shape[1], LANES), PLANE, 0, 0, tiled=True)
    own, other = sum_parts(parts, lax.axis_index("y_lo").astype(jnp.int32)[None], latent.shape)
    return (query_grad, join(own, swap(other, "y_lo"), query_grad))


def solution(mesh):
    fine = Mesh(mesh.devices.reshape(4, 2, 4, 2, 2), FINE_AXES)
    query, head = ("x", "y_lo"), ("z", "core")
    in_specs = (
        P(query, head, None),
        P(FINE_AXES, None),
        P(query, head, None),
        P(query, head),
        P(query, head),
    )
    out_specs = (P(query + ("y_hi",), head, None), P(FINE_AXES, None))
    return jax.shard_map(on_device, mesh=fine, in_specs=in_specs, out_specs=out_specs, check_vma=False)
```

```python
import functools
import math

import jax
import jax.numpy as jnp
from jax import lax
from jax.experimental import pallas as pl
from jax.experimental.pallas import tpu as pltpu
from jax.sharding import Mesh, PartitionSpec as P

softmax_scale = 192.0 ** (-0.5) * (0.1 * math.log(40.0) + 1.0) ** 2
log2_e = math.log2(math.e)

FINE_AXES = ("z", "core", "x", "y_lo", "y_hi")
CHIPS = ("z", "x", "y_lo")
PLANE = ("z", "x")
TILE = 512
LANES = 128
PIECES = 4

NT = (((1,), (1,)), ((), ()))
NN = (((1,), (0,)), ((), ()))
VMEM = pl.BlockSpec(memory_space=pltpu.VMEM)
HBM = pl.BlockSpec(memory_space=pl.ANY)


def f32_dot(left, right, dims):
    return lax.dot_general(left, right, dims, preferred_element_type=jnp.float32)


def in_vmem(array):
    return pltpu.with_memory_space_constraint(array, pltpu.VMEM)


def in_hbm(array):
    return pltpu.with_memory_space_constraint(array, pltpu.HBM)


def core_sum_kernel(mine_ref, theirs_ref, out_ref):
    out_ref[...] = (mine_ref[...] + theirs_ref[...]).astype(out_ref.dtype)


def core_sum(mine, theirs):
    return pl.pallas_call(
        core_sum_kernel,
        in_specs=[VMEM, VMEM],
        out_specs=VMEM,
        out_shape=pltpu.VMEM(mine.shape, jnp.bfloat16),
        compiler_params=pltpu.CompilerParams(vmem_limit_bytes=4 << 20),
        cost_estimate=pl.CostEstimate(flops=mine.size, bytes_accessed=mine.size, transcendentals=0),
        name="core_sum",
    )(in_vmem(mine), in_vmem(theirs))


def swap(array, axis):
    return lax.ppermute(array, axis, [(0, 1), (1, 0)])


def pack_kernel(latent_ref, packed_ref):
    shard, key_width = latent_ref.shape
    blocks = key_width // LANES
    for block in range(blocks):
        packed_ref[block * shard : (block + 1) * shard, :] = latent_ref[:, block * LANES : (block + 1) * LANES]
    rest = latent_ref[:, blocks * LANES :]
    packed_ref[blocks * shard :, :] = jnp.concatenate([rest[: shard // 2], rest[shard // 2 :]], axis=-1)


def pack(latent):
    return pl.pallas_call(
        pack_kernel,
        grid=(1,),
        in_specs=[pl.BlockSpec(latent.shape, lambda i: (0, 0))],
        out_specs=VMEM,
        out_shape=jax.ShapeDtypeStruct((latent.size // LANES, LANES), latent.dtype),
        compiler_params=pltpu.CompilerParams(vmem_limit_bytes=4 << 20),
        name="pack",
    )(in_hbm(latent))


def grads_kernel(first, last, stays, do_stays, n_halves, n_before, *refs):
    refs = list(refs)
    take = lambda number: [refs.pop(0) for _ in range(number)]
    half, key_ref, q_hbm, do_hbm, stat_ref = take(5)
    sum_in = [] if first else take(2)
    take(n_before)
    dq_refs = take(n_halves)
    dkv_ref = refs.pop(0) if last else None
    keys_ref = refs.pop(0) if first else key_ref
    key_acc, value_acc, q_tiles, sems, *refs = refs
    dkv_tiles = refs.pop() if last else None
    dq_tiles = [] if stays else [refs.pop(0)]
    do_tiles = refs
    rows, width = value_acc.shape
    key_width = keys_ref.shape[-1]
    count = dq_refs[0].shape[0]
    per_half = count // TILE

    def begin(tile):
        side = half[0] if tile < per_half else 1 - half[0]
        return pl.multiple_of(side * count, TILE) + tile % per_half * TILE

    copies, results = [], []
    for tile in range(n_halves * per_half):
        at = pl.ds(begin(tile), TILE)
        pair = [pltpu.make_async_copy(q_hbm.at[at, :], q_tiles.at[tile], sems.at[0, tile])]
        if not do_stays:
            pair.append(pltpu.make_async_copy(do_hbm.at[at, :], do_tiles[0].at[tile], sems.at[1, tile]))
        for copy in pair:
            copy.start()
        copies.append(pair)

    if first:
        blocks = width // LANES
        shards = key_ref.shape[0]
        shard = rows // shards
        for block in range(blocks):
            columns = key_ref[:, block * shard : (block + 1) * shard, :].reshape(rows, LANES)
            keys_ref[:, block * LANES : (block + 1) * LANES] = columns
        rest = key_ref[:, blocks * shard :, :]
        rest = jnp.stack([rest[:, :, : LANES // 2], rest[:, :, LANES // 2 :]], axis=1)
        keys_ref[:, width:] = rest.reshape(rows, key_width - width)
    keys = keys_ref[...]
    keys_t = keys.T
    for tile, pair in enumerate(copies):
        for copy in pair:
            copy.wait()
        queries = q_tiles[tile]
        douts = do_hbm[pl.ds(begin(tile), TILE), :] if do_stays else do_tiles[0][tile]
        side = half[0] if tile < per_half else 1 - half[0]
        stats = stat_ref[side * per_half + tile % per_half]
        scores = f32_dot(keys, queries, NT)
        dprobs = f32_dot(keys[:, :width], douts, NT)
        probs = jnp.exp2(scores * (softmax_scale * log2_e) - stats[0:1, :] * log2_e)
        dscores = (probs * (dprobs - stats[1:2, :])).astype(jnp.bfloat16)
        dq_at = dq_refs[tile // per_half].at[pl.ds(tile % per_half * TILE, TILE), :]
        query_part = f32_dot(keys_t, dscores, NN).T
        if stays:
            dq_at[...] = query_part
        else:
            dq_tiles[0][tile] = query_part
            result = pltpu.make_async_copy(dq_tiles[0].at[tile], dq_at, sems.at[2, tile])
            result.start()
            results.append(result)
        key_part = f32_dot(queries.T, dscores, NT)
        value_part = f32_dot(probs.astype(jnp.bfloat16), douts, NN)
        if tile > 0:
            key_acc[...] += key_part
            value_acc[...] += value_part
        elif first:
            key_acc[...] = key_part
            value_acc[...] = value_part
        else:
            key_acc[...] = sum_in[0][...] + key_part
            value_acc[...] = sum_in[1][...] + value_part
        if last and tile == len(copies) - 1:
            some = dkv_tiles.shape[0] // PIECES
            for piece in range(PIECES):
                shards = pl.ds(piece * some, some)
                at = slice(piece * rows // PIECES, (piece + 1) * rows // PIECES)
                shard = rows // dkv_tiles.shape[0]
                key_sum = key_acc[:, at].T * softmax_scale
                summed = (key_sum[:, :width] + value_acc[at, :]).astype(dkv_tiles.dtype)
                for block in range(width // LANES):
                    columns = summed[:, block * LANES : (block + 1) * LANES].reshape(some, shard, LANES)
                    dkv_tiles[shards, block * shard : (block + 1) * shard, :] = columns
                rest = key_sum[:, width:].astype(dkv_tiles.dtype).reshape(some, 2, shard // 2, LANES // 2)
                rest = jnp.concatenate([rest[:, 0], rest[:, 1]], axis=-1)
                dkv_tiles[shards, width // LANES * shard :, :] = rest
                result = pltpu.make_async_copy(dkv_tiles.at[shards], dkv_ref.at[shards], sems.at[3, piece])
                result.start()
                results.append(result)
    for result in results:
        result.wait()


def grads(keys, half, side, halves=1, sums=None, shards=0, stays=False, do_stays=False, before=()):
    queries, douts, stats = side
    key_width = queries.shape[1]
    rows = keys.size // key_width
    total, width = douts.shape
    count = total // 2
    tiles = halves * count // TILE
    first, last = sums is None, shards > 0
    operands = [half, in_vmem(keys), in_hbm(queries), (in_vmem if do_stays else in_hbm)(douts), in_vmem(stats)]
    in_specs = [VMEM, HBM, VMEM if do_stays else HBM, VMEM]
    sum_shapes = [(key_width, rows), (rows, width)]
    out_shape = [(pltpu.VMEM if stays else pltpu.HBM)((count, key_width), jnp.float32)] * halves
    out_specs = [VMEM if stays else HBM] * halves
    scratch = [
        pltpu.VMEM((tiles, TILE, key_width), queries.dtype),
        pltpu.SemaphoreType.DMA((4, max(tiles, PIECES))),
    ]
    if not stays:
        scratch.append(pltpu.VMEM((tiles, TILE, key_width), jnp.float32))
    if not do_stays:
        scratch.append(pltpu.VMEM((tiles, TILE, width), douts.dtype))
    aliases = {}
    if not first:
        if not last:
            aliases = {len(operands): halves, len(operands) + 1: halves + 1}
        operands += [in_vmem(array) for array in sums]
        in_specs += [VMEM, VMEM]
    if last:
        packed = (shards, rows // shards * key_width // LANES, LANES)
        out_shape.append(pltpu.HBM(packed, keys.dtype))
        out_specs.append(HBM)
        scratch = [pltpu.VMEM(shape, jnp.float32) for shape in sum_shapes] + scratch
        scratch.append(pltpu.VMEM(packed, keys.dtype))
    else:
        if first:
            out_shape.append(pltpu.VMEM((rows, key_width), keys.dtype))
            out_specs.append(VMEM)
        out_shape += [pltpu.VMEM(shape, jnp.float32) for shape in sum_shapes]
        out_specs += [VMEM, VMEM]
    place, spec = (in_hbm, HBM) if first else (in_vmem, VMEM)
    operands += [place(array) for array in before]
    in_specs += [spec] * len(before)
    return pl.pallas_call(
        functools.partial(grads_kernel, first, last, stays, do_stays, halves, len(before)),
        grid_spec=pltpu.PrefetchScalarGridSpec(
            num_scalar_prefetch=1, grid=(1,), in_specs=in_specs, out_specs=out_specs, scratch_shapes=scratch
        ),
        out_shape=out_shape,
        input_output_aliases=aliases,
        compiler_params=pltpu.CompilerParams(vmem_limit_bytes=32 << 20),
        cost_estimate=pl.CostEstimate(flops=rows * count, bytes_accessed=rows * key_width * 2, transcendentals=rows),
        name="grads",
    )(*operands)


def add_kernel(out_scale, *refs):
    *addends, out_ref = refs
    rows = out_ref.shape[0]
    at = pl.ds(pl.program_id(0) * rows, rows)
    parts = [addend[...] if addend.shape[0] == rows else addend[at] for addend in addends]
    total = parts[0].astype(jnp.float32)
    for part in parts[1:]:
        total += part.astype(jnp.float32)
    out_ref[...] = (total * out_scale if out_scale else total).astype(out_ref.dtype)


def add(addends, dtype, out_scale=None, resident=None):
    rows, heads, key_width = addends[0].shape
    steps = 2
    resident = resident or [True] * len(addends)
    block = pl.BlockSpec((rows // steps, heads, key_width), lambda i: (i, 0, 0))
    return pl.pallas_call(
        functools.partial(add_kernel, out_scale),
        grid=(steps,),
        in_specs=[VMEM if stays else block for stays in resident],
        out_specs=block,
        out_shape=pltpu.HBM((rows, heads, key_width), dtype),
        compiler_params=pltpu.CompilerParams(vmem_limit_bytes=12 << 20),
        cost_estimate=pl.CostEstimate(
            flops=rows * heads * key_width * 2, bytes_accessed=rows * heads * key_width * 4, transcendentals=0
        ),
        name="add",
    )(*[(in_vmem if stays else in_hbm)(addend) for addend, stays in zip(addends, resident)])


def sum_kernel(place, parts_ref, mine_ref, other_ref):
    shard, key_width = mine_ref.shape
    packed = parts_ref.shape[1] // 2
    blocks = key_width // LANES
    for out_ref, at in ((mine_ref, place[0]), (other_ref, 1 - place[0])):
        rows = pl.ds(pl.multiple_of(at * packed, shard // 2), packed)
        total = parts_ref[0, rows, :].astype(jnp.float32)
        for part in range(1, parts_ref.shape[0]):
            total += parts_ref[part, rows, :].astype(jnp.float32)
        for block in range(blocks):
            out_ref[:, block * LANES : (block + 1) * LANES] = total[block * shard : (block + 1) * shard, :]
        rest = total[blocks * shard :, :]
        out_ref[: shard // 2, blocks * LANES :] = rest[:, : LANES // 2]
        out_ref[shard // 2 :, blocks * LANES :] = rest[:, LANES // 2 :]


def sum_parts(parts, place, shape):
    return pl.pallas_call(
        sum_kernel,
        grid_spec=pltpu.PrefetchScalarGridSpec(num_scalar_prefetch=1, grid=(1,), in_specs=[VMEM], out_specs=[VMEM, VMEM]),
        out_shape=[pltpu.VMEM(shape, jnp.float32)] * 2,
        compiler_params=pltpu.CompilerParams(vmem_limit_bytes=4 << 20),
        name="sum_parts",
    )(place, in_vmem(parts))


def join_kernel(own_ref, other_ref, after_ref, out_ref):
    out_ref[...] = own_ref[...] + other_ref[...]


def join(own, other, after):
    return pl.pallas_call(
        join_kernel,
        in_specs=[VMEM, VMEM, HBM],
        out_specs=VMEM,
        out_shape=jax.ShapeDtypeStruct(own.shape, own.dtype),
        compiler_params=pltpu.CompilerParams(vmem_limit_bytes=4 << 20),
        name="join",
    )(in_vmem(own), in_vmem(other), in_hbm(after))


def on_device(queries, latent, out_grad, log_norms, row_dots):
    number, heads, key_width = queries.shape
    half = number // 2

    chips = lax.axis_size(CHIPS)
    packed = pack(latent)
    keys = lax.all_to_all(jnp.broadcast_to(packed[None], (chips, *packed.shape)), CHIPS, 0, 0, tiled=True)

    def flat(queries, out_grad, stats):
        rows = number * heads
        return (
            queries.reshape(rows, key_width),
            out_grad.reshape(rows, out_grad.shape[2]),
            stats.reshape(2, rows // TILE, TILE).transpose(1, 0, 2),
        )

    mine = (queries, out_grad, jnp.stack([log_norms, row_dots]))
    theirs = flat(*[swap(array, "core") for array in mine])
    mine = flat(*mine)

    kept = lax.axis_index("y_hi").astype(jnp.int32)[None]
    sent = 1 - kept
    whole = (half, heads, key_width)
    dq_sent_theirs, dq_theirs, keys, *sums = grads(keys, sent, theirs, halves=2, do_stays=True, before=mine)
    returned = swap(dq_sent_theirs.reshape(whole), "core")
    dq_sent_mine, *sums = grads(keys, sent, mine, sums=sums, stays=True)
    over_cores = core_sum(dq_sent_mine.reshape(whole), returned)
    received = swap(over_cores, "y_hi")
    dq_mine, dkv = grads(keys, kept, mine, sums=sums, shards=chips, before=[over_cores])
    returned = swap(dq_theirs.reshape(whole), "core")
    query_grad = add([dq_mine.reshape(whole), returned, received], jnp.float32, softmax_scale, resident=[False, False, True])
    parts = lax.all_to_all(dkv.reshape(-1, 2 * dkv.shape[1], LANES), PLANE, 0, 0, tiled=True)
    own, other = sum_parts(parts, lax.axis_index("y_lo").astype(jnp.int32)[None], latent.shape)
    return (query_grad, join(own, swap(other, "y_lo"), query_grad))


def solution(mesh):
    fine = Mesh(mesh.devices.reshape(4, 2, 4, 2, 2), FINE_AXES)
    query, head = ("x", "y_lo"), ("z", "core")
    in_specs = (
        P(query, head, None),
        P(FINE_AXES, None),
        P(query, head, None),
        P(query, head),
        P(query, head),
    )
    out_specs = (P(query + ("y_hi",), head, None), P(FINE_AXES, None))
    return jax.shard_map(on_device, mesh=fine, in_specs=in_specs, out_specs=out_specs, check_vma=False)
```
